256 devices in a mesh: row: 8 (over z_hi, core), col: 32 (over x, y, z_lo).
Axes of the slice: x: 4, y: 4, z: 8 (z_hi: 4, z_lo: 2; z = z_hi * 2 + z_lo), core: 2. Of those that a mesh axis runs over, the one named last changes fastest.
Arguments:
- object_field: float32 [2, 2, 2048, 8192], P(None, None, 'row', 'col'), may hold values from -5 to 5
- probe: float32 [2, 256, 256], replicated, may hold values from -5 to 5
- phase: float32 [256, 256], replicated, may hold values from -3.140625 to 3.140625
- amplitudes: float32 [8, 32, 1, 256, 256], P('row', 'col'), may hold values from 0.2 to 3
- offsets: int32 [8, 32, 1, 2], P('row', 'col'), may hold values from 0 to 128, as said below
Outputs:
- object_grad: float32 [2, 2, 2048, 8192], P(None, None, 'row', 'col')
- probe_grad: float32 [2, 256, 256], replicated
The draws below stay inside these ranges and needn't reach their ends.
Inputs may be any that keep to these rules, and one draw needn't show every extreme that they name: `offsets`: every offset lies between 0 and 128; in every draw some offset is 0 and some offset is 128.
All inputs are finite; a program needn't handle non-finite values.
Results may differ from the reference program's by a relative error of at most 0.0003.
Values sent between devices are 32-bit elements; how exact they have to be, the bound alone decides.
A program may use at most 64 MiB of HBM per device.

```python
import math
import jax
import jax.numpy as jnp
from jax import lax

N = 256
POS = 1
HALO = 64
GRID_R = 8
GRID_C = 32
HEIGHT = 2048
WIDTH = 8192


def draw_offsets(key, part):
    total = GRID_R * GRID_C * POS * 2
    values = jax.random.randint(key, (total,), 0, 2 * HALO + 1, dtype=jnp.int32)
    order = jax.random.permutation(jax.random.fold_in(key, 7), total)
    values = values.at[order[0]].set(0)
    values = values.at[order[1]].set(2 * HALO)
    return values.reshape(GRID_R, GRID_C, POS, 2).astype(jnp.int32)


def level_of(stream_key, shape, split, smallest, largest):
    factor_of, own = 1.0, jax.random.fold_in(stream_key, 6)
    for dim, parts in split:
        draws = jnp.exp(jax.random.uniform(jax.random.fold_in(own, dim), (parts,), jnp.float32, smallest / len(split), largest / len(split)))
        factor_of = factor_of * jnp.repeat(draws, shape[dim] // parts).reshape([-1 if axis == dim else 1 for axis in range(len(shape))])
    return factor_of


def noise(stream_key, dims, deviation, bound, cuts=(), kind=jnp.bfloat16):
    entries = deviation * jax.random.normal(stream_key, dims, jnp.float32)
    if cuts:
        entries = entries * level_of(stream_key, dims, cuts, -0.22, 0.18)
    return jnp.clip(entries, -bound, bound).astype(kind)


def setup_inputs(seed: int = 0) -> dict:
    splits = jax.random.split(jax.random.key(seed), 6)
    object_field = noise(splits[0], (2, 2, HEIGHT, WIDTH), 0.7, 5.0, ((2, 8), (3, 32)), jnp.float32)
    probe = noise(splits[1], (2, N, N), 0.7, 5.0, (), jnp.float32)
    phase = jnp.clip(jax.random.uniform(splits[2], (N, N), jnp.float32, -3.140625, 3.140625), -3.140625, 3.140625)
    amplitudes = jnp.clip(jnp.exp(math.log(3.0) - 2.7080502 * jax.random.uniform(splits[3], (GRID_R, GRID_C, POS, N, N), jnp.float32) ** level_of(splits[3], (GRID_R, GRID_C, POS, N, N), ((0, 8), (1, 32)), -0.2, 0.2)), 0.2, 3.0)
    offsets = draw_offsets(jax.random.fold_in(splits[5], 71), 0)
    return {"object_field": object_field, "probe": probe, "phase": phase, "amplitudes": amplitudes, "offsets": offsets}


EPS_AMP = 0.5

def dft_tables(count):
    counter = jnp.arange(count, dtype=jnp.int32)
    product_idx = counter[:, None] * counter[None, :] % count
    angles = product_idx.astype(jnp.float32) * (2.0 * jnp.pi / count)
    scale = 1.0 / jnp.sqrt(jnp.asarray(count, jnp.float32))
    return (jnp.cos(angles) * scale, -jnp.sin(angles) * scale)

def left_mult(table, field):
    return jnp.einsum('jk,...kl->...jl', table, field, precision=lax.Precision.HIGHEST)

def right_mult(field, table):
    return jnp.einsum('...jk,kl->...jl', field, table, precision=lax.Precision.HIGHEST)

def transform(real_part, imag_part, table_re, table_im):
    mid_re = left_mult(table_re, real_part) - left_mult(table_im, imag_part)
    mid_im = left_mult(table_re, imag_part) + left_mult(table_im, real_part)
    out_re = right_mult(mid_re, table_re) - right_mult(mid_im, table_im)
    out_im = right_mult(mid_im, table_re) + right_mult(mid_re, table_im)
    return (out_re, out_im)

def product(first_re, first_im, second_re, second_im):
    return (first_re * second_re - first_im * second_im, first_re * second_im + first_im * second_re)

def conj_product(first_re, first_im, second_re, second_im):
    return (first_re * second_re + first_im * second_im, first_re * second_im - first_im * second_re)

def position_grads(first_re, first_im, second_re, second_im, probe_re, probe_im, kernel_re, kernel_im, measured, table_re, table_im):
    entry = product(probe_re, probe_im, first_re, first_im)
    spectrum = transform(entry[0], entry[1], table_re, table_im)
    moved = product(kernel_re, kernel_im, spectrum[0], spectrum[1])
    arrive = transform(moved[0], moved[1], table_re, -table_im)
    leaving = product(arrive[0], arrive[1], second_re, second_im)
    far = transform(leaving[0], leaving[1], table_re, table_im)
    modulus = jnp.sqrt(far[0] * far[0] + far[1] * far[1] + EPS_AMP)
    factor = 2.0 * (1.0 - measured / modulus)
    back_far = transform(factor * far[0], factor * far[1], table_re, -table_im)
    grad_second = conj_product(arrive[0], arrive[1], back_far[0], back_far[1])
    back_arrive = conj_product(second_re, second_im, back_far[0], back_far[1])
    back_spec = transform(back_arrive[0], back_arrive[1], table_re, table_im)
    back_moved = conj_product(kernel_re, kernel_im, back_spec[0], back_spec[1])
    back_entry = transform(back_moved[0], back_moved[1], table_re, -table_im)
    grad_probe = conj_product(first_re, first_im, back_entry[0], back_entry[1])
    grad_first = conj_product(probe_re, probe_im, back_entry[0], back_entry[1])
    return (grad_first, grad_second, grad_probe)

def reference(object_field, probe, phase, amplitudes, offsets):
    table_re, table_im = dft_tables(N)
    kernel_re = jnp.cos(phase)
    kernel_im = jnp.sin(phase)
    height = object_field.shape[2]
    width = object_field.shape[3]
    padded = jnp.pad(object_field.reshape(4, height, width), ((0, 0), (HALO, HALO), (HALO, HALO)))
    flat_offsets = offsets.reshape(-1, 2)
    flat_amps = amplitudes.reshape(-1, N, N)
    total = flat_offsets.shape[0]

    def step(carry, index):
        grad_pad, grad_probe = carry
        tile_row = index // (GRID_C * POS)
        tile_col = index // POS % GRID_C
        start_y = (tile_row * N + flat_offsets[index, 0]).astype(jnp.int32)
        start_x = (tile_col * N + flat_offsets[index, 1]).astype(jnp.int32)
        zero = jnp.zeros((), jnp.int32)
        window = lax.dynamic_slice(padded, (zero, start_y, start_x), (4, N, N))
        measured = lax.dynamic_index_in_dim(flat_amps, index, 0, keepdims=False)
        grad_first, grad_second, grad_pr = position_grads(window[0], window[1], window[2], window[3], probe[0], probe[1], kernel_re, kernel_im, measured, table_re, table_im)
        piece = jnp.stack([grad_first[0], grad_first[1], grad_second[0], grad_second[1]])
        current = lax.dynamic_slice(grad_pad, (zero, start_y, start_x), (4, N, N))
        grad_pad = lax.dynamic_update_slice(grad_pad, current + piece, (zero, start_y, start_x))
        grad_probe = grad_probe + jnp.stack([grad_pr[0], grad_pr[1]])
        return ((grad_pad, grad_probe), None)
    init = (jnp.zeros(padded.shape, jnp.float32), jnp.zeros((2, N, N), jnp.float32))
    (grad_pad, grad_probe), leftover = lax.scan(step, init, jnp.arange(total, dtype=jnp.int32))
    object_grad = grad_pad[:, HALO:HALO + height, HALO:HALO + width].reshape(2, 2, height, width)
    return (object_grad, grad_probe)
```

```python
import functools

import jax
import jax.numpy as jnp
import ml_dtypes
import numpy as np
from jax import lax
from jax.experimental import pallas as pl
from jax.experimental.pallas import tpu as pltpu
from jax.sharding import PartitionSpec as P

EPS_AMP = 0.5
MESH = pl.DeviceIdType.MESH
N = 256
HALF = N // 2
MARGIN = 64
EXT = N + 2 * MARGIN
F32 = jnp.float32
BF16 = jnp.bfloat16

STEPS = ((-1, 0), (1, 0), (0, -1), (0, 1), (-1, -1), (-1, 1), (1, -1), (1, 1))


def dft_constants():
    j = np.arange(HALF)[:, None]
    k = np.arange(HALF)[None, :]
    mats = []
    for odd in (0, 1):
        angle = -2.0 * np.pi * (((2 * j + odd) * k) % N) / N
        re, im = np.cos(angle) / 16.0, np.sin(angle) / 16.0
        mats.append(np.block([[re, -im], [im, re]]))
    mats += [mats[0].T, mats[1].T]
    out = []
    for m in mats:
        hi = m.astype(ml_dtypes.bfloat16)
        lo = (m - hi.astype(np.float64)).astype(ml_dtypes.bfloat16)
        out.append(np.concatenate([hi, lo], axis=0))
    return np.stack(out)


def order_constant():
    q = np.zeros((N, N), np.float32)
    q[np.arange(HALF), 2 * np.arange(HALF)] = 1.0
    q[HALF + np.arange(HALF), 2 * np.arange(HALF) + 1] = 1.0
    return np.stack([q, q.T]).astype(ml_dtypes.bfloat16)


def dot(a, b):
    return jnp.dot(a, b, preferred_element_type=F32)


def two_terms(x):
    hi = x.astype(BF16)
    return hi, (x - hi.astype(F32)).astype(BF16)


def left_apply(table, x):
    hi, lo = two_terms(x)
    both = dot(table[...], hi)
    return both[:N] + both[N:] + dot(table[:N], lo)


def right_apply(x, table):
    hi, lo = two_terms(x)
    return dot(hi, table[:N]) + dot(lo, table[:N]) + dot(hi, table[N:])


def left_forward(x_re, x_im, tabs):
    low = jnp.concatenate([x_re[:HALF], x_im[:HALF]], axis=0)
    high = jnp.concatenate([x_re[HALF:], x_im[HALF:]], axis=0)
    even = left_apply(tabs.at[0], low + high)
    odd = left_apply(tabs.at[1], low - high)
    return (
        jnp.concatenate([even[:HALF], odd[:HALF]], axis=0),
        jnp.concatenate([even[HALF:], odd[HALF:]], axis=0),
    )


def right_forward(x_re, x_im, tabs):
    low = jnp.concatenate([x_re[:, :HALF], x_im[:, :HALF]], axis=1)
    high = jnp.concatenate([x_re[:, HALF:], x_im[:, HALF:]], axis=1)
    even = right_apply(low + high, tabs.at[2])
    odd = right_apply(low - high, tabs.at[3])
    return (
        jnp.concatenate([even[:, :HALF], odd[:, :HALF]], axis=1),
        jnp.concatenate([even[:, HALF:], odd[:, HALF:]], axis=1),
    )


def left_inverse(x_re, x_im, tabs):
    a = left_apply(tabs.at[2], jnp.concatenate([x_re[:HALF], x_im[:HALF]], axis=0))
    b = left_apply(tabs.at[3], jnp.concatenate([x_re[HALF:], x_im[HALF:]], axis=0))
    low, high = a + b, a - b
    return (
        jnp.concatenate([low[:HALF], high[:HALF]], axis=0),
        jnp.concatenate([low[HALF:], high[HALF:]], axis=0),
    )


def right_inverse(x_re, x_im, tabs):
    a = right_apply(jnp.concatenate([x_re[:, :HALF], x_im[:, :HALF]], axis=1), tabs.at[0])
    b = right_apply(jnp.concatenate([x_re[:, HALF:], x_im[:, HALF:]], axis=1), tabs.at[1])
    low, high = a + b, a - b
    return (
        jnp.concatenate([low[:, :HALF], high[:, :HALF]], axis=1),
        jnp.concatenate([low[:, HALF:], high[:, HALF:]], axis=1),
    )


def forward(x_re, x_im, tabs):
    return right_forward(*left_forward(x_re, x_im, tabs), tabs)


def inverse(x_re, x_im, tabs):
    return right_inverse(*left_inverse(x_re, x_im, tabs), tabs)


def product(a_re, a_im, b_re, b_im):
    return a_re * b_re - a_im * b_im, a_re * b_im + a_im * b_re


def conj_product(a_re, a_im, b_re, b_im):
    return a_re * b_re + a_im * b_im, a_re * b_im - a_im * b_re


def reorder(x, order):
    hi = x.astype(BF16)
    rest = x - hi.astype(F32)
    mid = rest.astype(BF16)
    low = (rest - mid.astype(F32)).astype(BF16)
    parts = []
    for term in (hi, mid, low):
        rows = dot(order[0], term).astype(BF16)
        parts.append(dot(rows, order[1]))
    return parts[0] + parts[1] + parts[2]


def cos_sin(x):
    h = 0.5 * x
    t = h * h
    s = h * (1.0 + t * (-1.0 / 6 + t * (1.0 / 120 + t * (-1.0 / 5040 + t * (
        1.0 / 362880 + t * (-1.0 / 39916800 + t * (1.0 / 6227020800)))))))
    c = 1.0 + t * (-0.5 + t * (1.0 / 24 + t * (-1.0 / 720 + t * (1.0 / 40320 + t * (
        -1.0 / 3628800 + t * (1.0 / 479001600 + t * (-1.0 / 87178291200)))))))
    return 1.0 - 2.0 * s * s, 2.0 * s * c


def kernel(
    rows, cols,
    obj, probe_in, phase_in, amp_in, offs, tabs_in, order_in,
    obj_out, probe_out,
    mid, side, pack, probe, phase, amp, tabs, order, win1, win2, arrive, kern,
    gmid, gside, rrow, rcol, rcor, gprobe, recv_a, half, recv_b, sum_b, recv_c, final, owned,
    in_sem, halo_send, halo_recv, fold_send, fold_recv, ar_send, ar_recv, out_sem,
):
    row, col = lax.axis_index("row"), lax.axis_index("col")
    core, z_hi = row % 2, row // 2
    plane, z_lo = col // 2, col % 2
    planes, zs = cols // 2, rows
    z = z_hi * 2 + z_lo
    share = N // planes

    def neighbour(step):
        return ((row + step[0] + rows) % rows, (col + step[1] + cols) % cols)

    partner = (z_hi * 2 + 1 - core, col)

    def plane_peer(d):
        return (row, ((plane + d) % planes) * 2 + z_lo)

    def z_peer(d):
        other = (z + d) % zs
        return ((other // 2) * 2 + core, plane * 2 + other % 2)

    loads = [
        pltpu.make_async_copy(obj.at[0], mid.at[0, :, pl.ds(MARGIN, N), :], in_sem.at[0]),
        pltpu.make_async_copy(obj.at[1], mid.at[1, :, pl.ds(MARGIN, N), :], in_sem.at[1]),
        pltpu.make_async_copy(probe_in, probe, in_sem.at[2]),
        pltpu.make_async_copy(phase_in, phase, in_sem.at[3]),
        pltpu.make_async_copy(order_in, order, in_sem.at[4]),
        pltpu.make_async_copy(amp_in.at[0, 0, 0], amp, in_sem.at[5]),
        pltpu.make_async_copy(tabs_in, tabs, in_sem.at[6]),
    ]
    for load in loads:
        load.start()

    barrier = pltpu.get_barrier_semaphore()
    for step in STEPS:
        pl.semaphore_signal(barrier, inc=1, device_id=neighbour(step), device_id_type=MESH)

    @pl.loop(1, planes)
    def _(d):
        pl.semaphore_signal(barrier, inc=1, device_id=plane_peer(d), device_id_type=MESH)

    @pl.loop(1, zs)
    def _(d):
        pl.semaphore_signal(barrier, inc=1, device_id=z_peer(d), device_id_type=MESH)

    lane = lax.broadcasted_iota(jnp.int32, (N, HALF), 1)
    lower = lane < 64

    def pack_sides(s):
        re, im = mid.at[s, 0], mid.at[s, 1]
        inner = pl.ds(MARGIN, N)
        pack[s, 0] = jnp.where(lower, re[inner, :HALF], pltpu.roll(im[inner, :HALF], 64, 1))
        pack[s, 1] = jnp.where(lower, pltpu.roll(re[inner, HALF:], 64, 1), im[inner, HALF:])

    def halo_copies(s):
        copies = []
        for i, (dr, dc) in enumerate(STEPS):
            src_rows = {-1: pl.ds(MARGIN, MARGIN), 1: pl.ds(N, MARGIN), 0: pl.ds(MARGIN, N)}[dr]
            pack_rows = {-1: pl.ds(0, MARGIN), 1: pl.ds(N - MARGIN, MARGIN), 0: pl.ds(0, N)}[dr]
            dst_rows = {-1: pl.ds(MARGIN + N, MARGIN), 1: pl.ds(0, MARGIN), 0: pl.ds(MARGIN, N)}[dr]
            if dc == 0:
                src, dst = mid.at[s, :, src_rows, :], mid.at[s, :, dst_rows, :]
            else:
                which = (dc + 1) // 2
                src, dst = pack.at[s, which, pack_rows, :], side.at[s, 1 - which, dst_rows, :]
            copies.append(pltpu.make_async_remote_copy(
                src_ref=src, dst_ref=dst, send_sem=halo_send.at[s, i], recv_sem=halo_recv.at[s, i],
                device_id=neighbour((dr, dc)), device_id_type=MESH))
        return copies

    halos = [halo_copies(0), halo_copies(1)]
    loads[0].wait()
    pack_sides(0)
    pl.semaphore_wait(barrier, 8 + planes - 1 + zs - 1)
    for copy in halos[0]:
        copy.start()
    loads[1].wait()
    pack_sides(1)

    loads[3].wait()
    loads[4].wait()
    kern[0], kern[1] = cos_sin(reorder(phase[...], order))
    loads[5].wait()
    amp[...] = reorder(amp[...], order)
    loads[2].wait()
    loads[6].wait()

    off_y, off_x = offs[0, 0, 0, 0], offs[0, 0, 0, 1]
    shift = off_x - MARGIN

    def clear_edges(s):
        @pl.when(row == 0)
        def _():
            mid[s, :, :MARGIN, :] = jnp.zeros((2, MARGIN, N), F32)
            side[s, :, :MARGIN, :] = jnp.zeros((2, MARGIN, HALF), F32)

        @pl.when(row == rows - 1)
        def _():
            mid[s, :, MARGIN + N:EXT, :] = jnp.zeros((2, MARGIN, N), F32)
            side[s, :, MARGIN + N:EXT, :] = jnp.zeros((2, MARGIN, HALF), F32)

        @pl.when(col == 0)
        def _():
            side[s, 0, :EXT] = jnp.zeros((EXT, HALF), F32)

        @pl.when(col == cols - 1)
        def _():
            side[s, 1, :EXT] = jnp.zeros((EXT, HALF), F32)

    def rows_up(view, amount):
        return pltpu.roll(view[...], lax.rem(EXT - amount, EXT), 0)[:N]

    def window(s, ref):
        left, right = rows_up(side.at[s, 0], off_y), rows_up(side.at[s, 1], off_y)
        for part in (0, 1):
            both = rows_up(mid.at[s, part], off_y)
            low, high = both[:, :HALF], both[:, HALF:]
            from_right = right if part == 0 else pltpu.roll(right, 64, 1)
            from_left = pltpu.roll(left, 64, 1) if part == 0 else left
            low = jnp.where(lane < shift, from_right, low)
            high = jnp.where(lane >= HALF + shift, from_left, high)
            whole = jnp.concatenate([low, high], axis=1)
            ref[part] = pltpu.roll(whole, lax.rem(N + MARGIN - off_x, N), 1)

    def spread(s, g_re, g_im):
        zero = jnp.zeros((N, HALF), F32)

        def down(x):
            below = jnp.zeros((EXT - N, x.shape[1]), F32)
            return pltpu.roll(jnp.concatenate([x, below], axis=0), off_y, 0)

        lefts, rights = [], []
        for part, g in ((0, g_re), (1, g_im)):
            moved = pltpu.roll(g, lax.rem(off_x + N - MARGIN, N), 1)
            low, high = moved[:, :HALF], moved[:, HALF:]
            over_right, over_left = lane < shift, lane >= HALF + shift
            kept = [jnp.where(over_right, zero, low), jnp.where(over_left, zero, high)]
            gmid[s, part] = down(jnp.concatenate(kept, axis=1))
            rights.append(jnp.where(over_right, low, zero))
            lefts.append(jnp.where(over_left, high, zero))
        gside[s, 0] = down(jnp.where(lower, pltpu.roll(lefts[0], 64, 1), lefts[1]))
        gside[s, 1] = down(jnp.where(lower, rights[0], pltpu.roll(rights[1], 64, 1)))

    def fold_copies(s):
        copies = []
        for i, (dr, dc) in enumerate(STEPS):
            src_rows = {-1: pl.ds(0, MARGIN), 1: pl.ds(MARGIN + N, MARGIN), 0: pl.ds(MARGIN, N)}[dr]
            which = (dc + 1) // 2
            if dc == 0:
                src, dst = gmid.at[s, :, src_rows, :], rrow.at[s, i]
            elif dr == 0:
                src, dst = gside.at[s, which, src_rows, :], rcol.at[s, i - 2]
            else:
                src, dst = gside.at[s, which, src_rows, :], rcor.at[s, i - 4]
            copies.append(pltpu.make_async_remote_copy(
                src_ref=src, dst_ref=dst, send_sem=fold_send.at[s, i], recv_sem=fold_recv.at[s, i],
                device_id=neighbour((dr, dc)), device_id_type=MESH))
        return copies

    folds = [fold_copies(0), fold_copies(1)]

    has = {-1: row < rows - 1, 1: row > 0}
    has_col = {-1: col < cols - 1, 1: col > 0}

    def collect(s):
        for part in (0, 1):
            owned[s, part] = gmid[s, part, MARGIN:MARGIN + N, :]
        for i, dr in ((0, -1), (1, 1)):
            place = pl.ds(N - MARGIN, MARGIN) if dr == -1 else pl.ds(0, MARGIN)

            @pl.when(has[dr])
            def _():
                owned[s, :, place, :] += rrow[s, i]

        def add_side(got, place, count, dc):
            low = lower[:count]
            if dc == -1:
                re, im, lanes = jnp.where(low, 0.0, pltpu.roll(got, 64, 1)), jnp.where(low, 0.0, got), slice(HALF, N)
            else:
                re, im, lanes = jnp.where(low, got, 0.0), jnp.where(low, pltpu.roll(got, 64, 1), 0.0), slice(0, HALF)
            owned[s, 0, place, lanes] += re
            owned[s, 1, place, lanes] += im

        for i, (dr, dc) in enumerate(STEPS):
            if dc == 0:
                continue
            if dr == 0:
                @pl.when(has_col[dc])
                def _():
                    add_side(rcol[s, i - 2], pl.ds(0, N), N, dc)
            else:
                place = pl.ds(N - MARGIN, MARGIN) if dr == -1 else pl.ds(0, MARGIN)

                @pl.when(jnp.logical_and(has_col[dc], has[dr]))
                def _():
                    add_side(rcor[s, i - 4], place, MARGIN, dc)

    for copy in halos[0]:
        copy.wait_recv()
    for copy in halos[1]:
        copy.start()
    clear_edges(0)
    window(0, win1)
    entry = product(probe[0], probe[1], win1[0], win1[1])
    spectrum = forward(*entry, tabs)
    moved = product(kern[0], kern[1], *spectrum)
    arrive[0], arrive[1] = inverse(*moved, tabs)

    for copy in halos[1]:
        copy.wait_recv()
    clear_edges(1)
    window(1, win2)
    far_re, far_im = forward(*product(arrive[0], arrive[1], win2[0], win2[1]), tabs)
    factor = 2.0 - 2.0 * amp[...] * lax.rsqrt(far_re * far_re + far_im * far_im + EPS_AMP)
    back_re, back_im = inverse(factor * far_re, factor * far_im, tabs)
    spread(1, *conj_product(arrive[0], arrive[1], back_re, back_im))
    for copy in folds[1]:
        copy.start()
    spec = forward(*conj_product(win2[0], win2[1], back_re, back_im), tabs)
    ent_re, ent_im = inverse(*conj_product(kern[0], kern[1], *spec), tabs)
    gprobe[0], gprobe[1] = conj_product(win1[0], win1[1], ent_re, ent_im)

    pair = pltpu.make_async_remote_copy(
        src_ref=gprobe.at[1 - core], dst_ref=recv_a, send_sem=ar_send.at[0, 0], recv_sem=ar_recv.at[0, 0],
        device_id=partner, device_id_type=MESH)
    pair.start()
    spread(0, *conj_product(probe[0], probe[1], ent_re, ent_im))
    pair.wait_recv()
    half[...] = gprobe[core] + recv_a[...]

    def scatter(d):
        peer = (plane + d) % planes
        return pltpu.make_async_remote_copy(
            src_ref=half.at[pl.ds(pl.multiple_of(peer * share, share), share), :], dst_ref=recv_b.at[d],
            send_sem=ar_send.at[1, d], recv_sem=ar_recv.at[1, d], device_id=plane_peer(d), device_id_type=MESH)

    @pl.loop(1, planes)
    def _(d):
        scatter(d).start()

    for copy in folds[0]:
        copy.start()

    mine = pl.ds(pl.multiple_of(plane * share, share), share)
    recv_b[0] = half[mine, :]

    @pl.loop(1, planes)
    def _(d):
        scatter(d).wait_recv()

    total = recv_b[0]
    for d in range(1, planes):
        total = total + recv_b[d]
    sum_b[...] = total

    def across(d):
        return pltpu.make_async_remote_copy(
            src_ref=sum_b, dst_ref=recv_c.at[z], send_sem=ar_send.at[2, d], recv_sem=ar_recv.at[2, d],
            device_id=z_peer(d), device_id_type=MESH)

    @pl.loop(1, zs)
    def _(d):
        across(d).start()

    recv_c[z] = total

    for copy in folds[1]:
        copy.wait_recv()
    collect(1)
    store1 = pltpu.make_async_copy(owned.at[1], obj_out.at[1], out_sem.at[1])
    store1.start()

    @pl.loop(1, zs)
    def _(d):
        across(d).wait_recv()

    total = recv_c[0]
    for d in range(1, zs):
        total = total + recv_c[d]
    final[core, mine, :] = total

    def gather(d):
        return pltpu.make_async_remote_copy(
            src_ref=final.at[core, mine, :], dst_ref=final.at[core, mine, :],
            send_sem=ar_send.at[3, d], recv_sem=ar_recv.at[3, d], device_id=plane_peer(d), device_id_type=MESH)

    def hand_over(d):
        owner = (plane - d + planes) % planes
        place = final.at[core, pl.ds(pl.multiple_of(owner * share, share), share), :]
        return pltpu.make_async_remote_copy(
            src_ref=place, dst_ref=place, send_sem=ar_send.at[4, d], recv_sem=ar_recv.at[4, d],
            device_id=partner, device_id_type=MESH)

    @pl.loop(1, planes)
    def _(d):
        gather(d).start()

    hand_over(0).start()

    for copy in folds[0]:
        copy.wait_recv()
    collect(0)
    store0 = pltpu.make_async_copy(owned.at[0], obj_out.at[0], out_sem.at[0])
    store0.start()

    @pl.loop(1, planes)
    def _(d):
        gather(d).wait_recv()
        hand_over(d).start()

    @pl.loop(0, planes)
    def _(d):
        hand_over(d).wait_recv()

    store2 = pltpu.make_async_copy(final, probe_out, out_sem.at[2])
    store2.start()

    for group in halos + folds:
        for copy in group:
            copy.wait_send()
    pair.wait_send()
    hand_over(0).wait_send()

    @pl.loop(1, planes)
    def _(d):
        scatter(d).wait_send()
        gather(d).wait_send()
        hand_over(d).wait_send()

    @pl.loop(1, zs)
    def _(d):
        across(d).wait_send()

    store0.wait()
    store1.wait()
    store2.wait()


def body(rows, cols, object_field, probe, phase, amplitudes, offsets):
    planes, zs = cols // 2, rows
    share = N // planes
    vmem = lambda *shape: pltpu.VMEM(shape, F32)
    dma = pltpu.SemaphoreType.DMA
    hbm = pl.BlockSpec(memory_space=pl.ANY)
    return pl.pallas_call(
        functools.partial(kernel, rows, cols),
        out_shape=(
            jax.ShapeDtypeStruct((2, 2, N, N), F32),
            jax.ShapeDtypeStruct((2, N, N), F32),
        ),
        in_specs=[hbm, hbm, hbm, hbm, pl.BlockSpec(memory_space=pltpu.SMEM), hbm, hbm],
        out_specs=(hbm, hbm),
        scratch_shapes=[
            vmem(2, 2, EXT, N),
            vmem(2, 2, EXT, HALF),
            vmem(2, 2, N, HALF),
            vmem(2, N, N),
            vmem(N, N),
            vmem(N, N),
            pltpu.VMEM((4, 2 * N, N), BF16),
            pltpu.VMEM((2, N, N), BF16),
            vmem(2, N, N),
            vmem(2, N, N),
            vmem(2, N, N),
            vmem(2, N, N),
            vmem(2, 2, EXT, N),
            vmem(2, 2, EXT, HALF),
            vmem(2, 2, 2, MARGIN, N),
            vmem(2, 2, N, HALF),
            vmem(2, 4, MARGIN, HALF),
            vmem(2, N, N),
            vmem(N, N),
            vmem(N, N),
            vmem(planes, share, N),
            vmem(share, N),
            vmem(zs, share, N),
            vmem(2, N, N),
            vmem(2, 2, N, N),
            dma((7,)),
            dma((2, 8)),
            dma((2, 8)),
            dma((2, 8)),
            dma((2, 8)),
            dma((5, 16)),
            dma((5, 16)),
            dma((3,)),
        ],
        compiler_params=pltpu.CompilerParams(
            collective_id=0, has_side_effects=True, vmem_limit_bytes=48 * 1024 * 1024
        ),
    )(object_field, probe, phase, amplitudes, offsets, jnp.asarray(dft_constants()), jnp.asarray(order_constant()))


def solution(mesh):
    placed = (
        P(None, None, "row", "col"),
        P(),
        P(),
        P("row", "col", None, None, None),
        P("row", "col", None, None),
    )
    return jax.shard_map(
        functools.partial(body, mesh.shape["row"], mesh.shape["col"]),
        mesh=mesh,
        in_specs=placed,
        out_specs=(P(None, None, "row", "col"), P()),
        check_vma=False,
    )
```

```python
import functools

import jax
import jax.numpy as jnp
import ml_dtypes
import numpy as np
from jax import lax
from jax.experimental import pallas as pl
from jax.experimental.pallas import tpu as pltpu
from jax.sharding import PartitionSpec as P

EPS_AMP = 0.5
MESH = pl.DeviceIdType.MESH
N = 256
HALF = N // 2
MARGIN = 64
EXT = N + 2 * MARGIN
F32 = jnp.float32
BF16 = jnp.bfloat16


def dft_constants():
    j = np.arange(HALF)[:, None]
    k = np.arange(HALF)[None, :]
    mats = []
    for odd in (0, 1):
        angle = -2.0 * np.pi * (((2 * j + odd) * k) % N) / N
        re, im = np.cos(angle) / 16.0, np.sin(angle) / 16.0
        mats.append(np.block([[re, -im], [im, re]]))
    mats += [mats[0].T, mats[1].T]
    out = []
    for m in mats:
        hi = m.astype(ml_dtypes.bfloat16)
        lo = (m - hi.astype(np.float64)).astype(ml_dtypes.bfloat16)
        out.append(np.concatenate([hi, lo], axis=0))
    return np.stack(out)


def order_constant():
    q = np.zeros((N, N), np.float32)
    q[np.arange(HALF), 2 * np.arange(HALF)] = 1.0
    q[HALF + np.arange(HALF), 2 * np.arange(HALF) + 1] = 1.0
    return np.stack([q, q.T]).astype(ml_dtypes.bfloat16)


def dot(a, b):
    return jnp.dot(a, b, preferred_element_type=F32)


def two_terms(x):
    hi = x.astype(BF16)
    return hi, (x - hi.astype(F32)).astype(BF16)


def left_apply(table, x):
    hi, lo = two_terms(x)
    both = dot(table[...], hi)
    return both[:N] + both[N:] + dot(table[:N], lo)


def right_apply(x, table):
    hi, lo = two_terms(x)
    return dot(hi, table[:N]) + dot(lo, table[:N]) + dot(hi, table[N:])


def left_forward(x_re, x_im, tabs):
    low = jnp.concatenate([x_re[:HALF], x_im[:HALF]], axis=0)
    high = jnp.concatenate([x_re[HALF:], x_im[HALF:]], axis=0)
    even = left_apply(tabs.at[0], low + high)
    odd = left_apply(tabs.at[1], low - high)
    return (
        jnp.concatenate([even[:HALF], odd[:HALF]], axis=0),
        jnp.concatenate([even[HALF:], odd[HALF:]], axis=0),
    )


def right_forward(x_re, x_im, tabs):
    low = jnp.concatenate([x_re[:, :HALF], x_im[:, :HALF]], axis=1)
    high = jnp.concatenate([x_re[:, HALF:], x_im[:, HALF:]], axis=1)
    even = right_apply(low + high, tabs.at[2])
    odd = right_apply(low - high, tabs.at[3])
    return (
        jnp.concatenate([even[:, :HALF], odd[:, :HALF]], axis=1),
        jnp.concatenate([even[:, HALF:], odd[:, HALF:]], axis=1),
    )


def left_inverse(x_re, x_im, tabs):
    a = left_apply(tabs.at[2], jnp.concatenate([x_re[:HALF], x_im[:HALF]], axis=0))
    b = left_apply(tabs.at[3], jnp.concatenate([x_re[HALF:], x_im[HALF:]], axis=0))
    low, high = a + b, a - b
    return (
        jnp.concatenate([low[:HALF], high[:HALF]], axis=0),
        jnp.concatenate([low[HALF:], high[HALF:]], axis=0),
    )


def right_inverse(x_re, x_im, tabs):
    a = right_apply(jnp.concatenate([x_re[:, :HALF], x_im[:, :HALF]], axis=1), tabs.at[0])
    b = right_apply(jnp.concatenate([x_re[:, HALF:], x_im[:, HALF:]], axis=1), tabs.at[1])
    low, high = a + b, a - b
    return (
        jnp.concatenate([low[:, :HALF], high[:, :HALF]], axis=1),
        jnp.concatenate([low[:, HALF:], high[:, HALF:]], axis=1),
    )


def forward(x_re, x_im, tabs):
    return right_forward(*left_forward(x_re, x_im, tabs), tabs)


def inverse(x_re, x_im, tabs):
    return right_inverse(*left_inverse(x_re, x_im, tabs), tabs)


def product(a_re, a_im, b_re, b_im):
    return a_re * b_re - a_im * b_im, a_re * b_im + a_im * b_re


def conj_product(a_re, a_im, b_re, b_im):
    return a_re * b_re + a_im * b_im, a_re * b_im - a_im * b_re


def reorder(x, order):
    hi = x.astype(BF16)
    rest = x - hi.astype(F32)
    mid = rest.astype(BF16)
    low = (rest - mid.astype(F32)).astype(BF16)
    parts = []
    for term in (hi, mid, low):
        rows = dot(order[0], term).astype(BF16)
        parts.append(dot(rows, order[1]))
    return parts[0] + parts[1] + parts[2]


def cos_sin(x):
    h = 0.5 * x
    t = h * h
    s = h * (1.0 + t * (-1.0 / 6 + t * (1.0 / 120 + t * (-1.0 / 5040 + t * (
        1.0 / 362880 + t * (-1.0 / 39916800 + t * (1.0 / 6227020800)))))))
    c = 1.0 + t * (-0.5 + t * (1.0 / 24 + t * (-1.0 / 720 + t * (1.0 / 40320 + t * (
        -1.0 / 3628800 + t * (1.0 / 479001600 + t * (-1.0 / 87178291200)))))))
    return 1.0 - 2.0 * s * s, 2.0 * s * c


def kernel(
    rows, cols,
    obj, probe_in, phase_in, amp_in, offs, tabs_in, order_in,
    obj_out, probe_out,
    mid, pack, hop, pick, side, probe, phase, amp, tabs, order, peer_offs, win1, win2, arrive, kern,
    gmid, gpick, gside, ghop, rrow, rhop, rcor, gprobe, recv_a, half, recv_b, sum_b, recv_c, final, owned,
    in_sem, offs_sem, halo_send, halo_recv, fold_send, fold_recv, ar_send, ar_recv, out_sem,
):
    row, col = lax.axis_index("row"), lax.axis_index("col")
    core, z_hi = row % 2, row // 2
    plane, z_lo = col // 2, col % 2
    planes, zs = cols // 2, rows
    z = z_hi * 2 + z_lo
    share = N // planes

    def neighbour(dr, dc):
        return ((row + dr + rows) % rows, (col + dc + cols) % cols)

    hop_to = 4 * z_lo - 2
    pair_peer = (row, col + 1 - 2 * z_lo)
    partner = (z_hi * 2 + 1 - core, col)

    def plane_peer(d):
        return (row, ((plane + d) % planes) * 2 + z_lo)

    def z_peer(d):
        other = (z + d) % zs
        return ((other // 2) * 2 + core, plane * 2 + other % 2)

    loads = [
        pltpu.make_async_copy(obj.at[0], mid.at[0, :, pl.ds(MARGIN, N), :], in_sem.at[0]),
        pltpu.make_async_copy(obj.at[1], mid.at[1, :, pl.ds(MARGIN, N), :], in_sem.at[1]),
        pltpu.make_async_copy(probe_in, probe, in_sem.at[2]),
        pltpu.make_async_copy(phase_in, phase, in_sem.at[3]),
        pltpu.make_async_copy(order_in, order, in_sem.at[4]),
        pltpu.make_async_copy(amp_in.at[0, 0, 0], amp, in_sem.at[5]),
        pltpu.make_async_copy(tabs_in, tabs, in_sem.at[6]),
    ]
    for load in loads:
        load.start()

    barrier = pltpu.get_barrier_semaphore()
    for step in ((-1, 0), (1, 0), (-1, -2), (-1, 2), (1, -2), (1, 2)):
        pl.semaphore_signal(barrier, inc=1, device_id=neighbour(*step), device_id_type=MESH)

    @pl.loop(1, planes)
    def _(d):
        pl.semaphore_signal(barrier, inc=1, device_id=plane_peer(d), device_id_type=MESH)

    @pl.loop(1, zs)
    def _(d):
        pl.semaphore_signal(barrier, inc=1, device_id=z_peer(d), device_id_type=MESH)

    lane = lax.broadcasted_iota(jnp.int32, (N, HALF), 1)
    lower = lax.broadcasted_iota(jnp.int32, (EXT, HALF), 1) < 64

    def left_margin(re, im):
        return jnp.where(lower[:re.shape[0]], re, pltpu.roll(im, 64, 1))

    def right_margin(re, im):
        return jnp.where(lower[:re.shape[0]], pltpu.roll(re, 64, 1), im)

    def pack_outer(s):
        inner = pl.ds(MARGIN, N)

        @pl.when(z_lo == 0)
        def _():
            pack[s] = left_margin(mid[s, 0, inner, :HALF], mid[s, 1, inner, :HALF])

        @pl.when(z_lo == 1)
        def _():
            pack[s] = right_margin(mid[s, 0, inner, HALF:], mid[s, 1, inner, HALF:])

    def remote(src, dst, send, recv, device):
        return pltpu.make_async_remote_copy(
            src_ref=src, dst_ref=dst, send_sem=send, recv_sem=recv, device_id=device, device_id_type=MESH)

    top, inner, bottom = pl.ds(0, MARGIN), pl.ds(MARGIN, N), pl.ds(MARGIN + N, MARGIN)

    def halo_hops(s):
        moves = (
            (pack.at[s], hop.at[s, inner, :], (0, hop_to)),
            (pack.at[s, pl.ds(0, MARGIN), :], hop.at[s, bottom, :], (-1, hop_to)),
            (pack.at[s, pl.ds(N - MARGIN, MARGIN), :], hop.at[s, top, :], (1, hop_to)),
        )
        return [remote(src, dst, halo_send.at[s, i], halo_recv.at[s, i], neighbour(*step))
                for i, (src, dst, step) in enumerate(moves)]

    def halo_rows(s):
        moves = (
            (mid.at[s, :, pl.ds(MARGIN, MARGIN), :], mid.at[s, :, bottom, :], (-1, 0)),
            (mid.at[s, :, pl.ds(N, MARGIN), :], mid.at[s, :, top, :], (1, 0)),
        )
        return [remote(src, dst, halo_send.at[s, 3 + i], halo_recv.at[s, 3 + i], neighbour(*step))
                for i, (src, dst, step) in enumerate(moves)]

    def halo_side(s):
        return remote(pick.at[s], side.at[s], halo_send.at[s, 5], halo_recv.at[s, 5], pair_peer)

    hops, halo_row, sides = ([f(s) for s in (0, 1)] for f in (halo_hops, halo_rows, halo_side))
    exchange = remote(offs, peer_offs, offs_sem.at[0], offs_sem.at[1], pair_peer)
    loads[0].wait()
    pack_outer(0)
    pl.semaphore_wait(barrier, 6 + planes - 1 + zs - 1)
    exchange.start()
    for copy in halo_row[0] + hops[0]:
        copy.start()
    loads[1].wait()
    pack_outer(1)
    hops[1][0].start()

    loads[3].wait()
    loads[4].wait()
    kern[0], kern[1] = cos_sin(reorder(phase[...], order))
    loads[5].wait()
    amp[...] = reorder(amp[...], order)
    loads[2].wait()
    loads[6].wait()

    off_y, off_x = offs[0, 0, 0, 0], offs[0, 0, 0, 1]
    shift = off_x - MARGIN

    outside = jnp.logical_or(
        jnp.logical_and(col == 0, off_x < MARGIN), jnp.logical_and(col == cols - 1, off_x > MARGIN))
    inside = 1.0 - outside.astype(F32)

    def clear_edges(s):
        @pl.when(row == 0)
        def _():
            mid[s, :, top, :] = jnp.zeros((2, MARGIN, N), F32)
            hop[s, top, :] = jnp.zeros((MARGIN, HALF), F32)

        @pl.when(row == rows - 1)
        def _():
            mid[s, :, bottom, :] = jnp.zeros((2, MARGIN, N), F32)
            hop[s, bottom, :] = jnp.zeros((MARGIN, HALF), F32)

    def up(x, amount):
        return pltpu.roll(x, lax.rem(EXT - amount, EXT), 0)[:N]

    def down(x, amount):
        below = jnp.zeros((EXT - N, x.shape[1]), F32)
        return pltpu.roll(jnp.concatenate([x, below], axis=0), amount, 0)

    def peer_takes_own(shape):
        reach = (peer_offs[0, 0, 0, 1] - MARGIN) * (1 - 2 * z_lo)
        return lax.broadcasted_iota(jnp.int32, shape, 1) * 0 + reach < 0

    def choose(s):
        own = peer_takes_own((EXT, HALF))

        @pl.when(z_lo == 0)
        def _():
            mine = right_margin(mid[s, 0, :, HALF:], mid[s, 1, :, HALF:])
            pick[s] = up(jnp.where(own, mine, hop[s]), peer_offs[0, 0, 0, 0])

        @pl.when(z_lo == 1)
        def _():
            mine = left_margin(mid[s, 0, :, :HALF], mid[s, 1, :, :HALF])
            pick[s] = up(jnp.where(own, mine, hop[s]), peer_offs[0, 0, 0, 0])

    over_right, over_left = lane < shift, lane >= HALF + shift

    def window(s, ref):
        beside = side[s] * inside
        turned = pltpu.roll(beside, 64, 1)
        for part in (0, 1):
            both = up(mid[s, part], off_y)
            low = jnp.where(over_right, beside if part == 0 else turned, both[:, :HALF])
            high = jnp.where(over_left, turned if part == 0 else beside, both[:, HALF:])
            ref[part] = pltpu.roll(jnp.concatenate([low, high], axis=1), lax.rem(N + MARGIN - off_x, N), 1)

    def spread(s, g_re, g_im):
        zero = jnp.zeros((N, HALF), F32)
        lefts, rights = [], []
        for part, g in ((0, g_re), (1, g_im)):
            moved = pltpu.roll(g, lax.rem(off_x + N - MARGIN, N), 1)
            low, high = moved[:, :HALF], moved[:, HALF:]
            rights.append(jnp.where(over_right, low, zero))
            lefts.append(jnp.where(over_left, high, zero))
            kept = [jnp.where(over_right, zero, low), jnp.where(over_left, zero, high)]
            gmid[s, part] = down(jnp.concatenate(kept, axis=1), off_y)
        gpick[s] = right_margin(*lefts) + left_margin(*rights)

    def fold_side(s):
        return remote(gpick.at[s], gside.at[s], fold_send.at[s, 5], fold_recv.at[s, 5], pair_peer)

    def fold_hops(s):
        moves = (
            (ghop.at[s, inner, :], rhop.at[s], (0, -hop_to)),
            (ghop.at[s, top, :], rcor.at[s, 0], (-1, -hop_to)),
            (ghop.at[s, bottom, :], rcor.at[s, 1], (1, -hop_to)),
        )
        return [remote(src, dst, fold_send.at[s, i], fold_recv.at[s, i], neighbour(*step))
                for i, (src, dst, step) in enumerate(moves)]

    def fold_rows(s):
        moves = (
            (gmid.at[s, :, top, :], rrow.at[s, 0], (-1, 0)),
            (gmid.at[s, :, bottom, :], rrow.at[s, 1], (1, 0)),
        )
        return [remote(src, dst, fold_send.at[s, 3 + i], fold_recv.at[s, 3 + i], neighbour(*step))
                for i, (src, dst, step) in enumerate(moves)]

    fsides, fhops, frows = ([f(s) for s in (0, 1)] for f in (fold_side, fold_hops, fold_rows))

    def add_packed(ref, s, place, packed, lefthand):
        low = lower[:packed.shape[0]]
        turned = pltpu.roll(packed, 64, 1)
        if lefthand:
            ref[s, 0, place, :HALF] += jnp.where(low, packed, 0.0)
            ref[s, 1, place, :HALF] += jnp.where(low, turned, 0.0)
        else:
            ref[s, 0, place, HALF:] += jnp.where(low, 0.0, turned)
            ref[s, 1, place, HALF:] += jnp.where(low, 0.0, packed)

    def pass_on(s):
        fsides[s].wait_recv()
        got = down(gside[s], peer_offs[0, 0, 0, 0])
        own = peer_takes_own((EXT, HALF))
        ghop[s] = jnp.where(own, 0.0, got)
        for copy in fhops[s]:
            copy.start()
        here = jnp.where(own, got, 0.0)

        @pl.when(z_lo == 0)
        def _():
            add_packed(gmid, s, pl.ds(0, EXT), here, False)

        @pl.when(z_lo == 1)
        def _():
            add_packed(gmid, s, pl.ds(0, EXT), here, True)

        for copy in frows[s]:
            copy.start()

    first, last = pl.ds(0, MARGIN), pl.ds(N - MARGIN, MARGIN)

    def collect(s):
        for copy in fhops[s] + frows[s]:
            copy.wait_recv()
        for part in (0, 1):
            owned[s, part] = gmid[s, part, inner, :]

        @pl.when(row < rows - 1)
        def _():
            owned[s, :, last, :] += rrow[s, 0]

        @pl.when(row > 0)
        def _():
            owned[s, :, first, :] += rrow[s, 1]

        for lo, valid in ((0, col > 0), (1, col < cols - 1)):
            @pl.when(jnp.logical_and(z_lo == lo, valid))
            def _():
                add_packed(owned, s, pl.ds(0, N), rhop[s], lo == 0)

                @pl.when(row < rows - 1)
                def _():
                    add_packed(owned, s, last, rcor[s, 0], lo == 0)

                @pl.when(row > 0)
                def _():
                    add_packed(owned, s, first, rcor[s, 1], lo == 0)

    exchange.wait_recv()
    for copy in halo_row[0] + hops[0]:
        copy.wait_recv()
    clear_edges(0)
    choose(0)
    sides[0].start()
    for copy in halo_row[1] + hops[1][1:]:
        copy.start()
    sides[0].wait_recv()
    window(0, win1)
    entry = product(probe[0], probe[1], win1[0], win1[1])
    spectrum = forward(*entry, tabs)
    moved = product(kern[0], kern[1], *spectrum)
    arrive[0], arrive[1] = inverse(*moved, tabs)

    for copy in halo_row[1] + hops[1]:
        copy.wait_recv()
    clear_edges(1)
    choose(1)
    sides[1].start()
    sides[1].wait_recv()
    window(1, win2)
    far_re, far_im = forward(*product(arrive[0], arrive[1], win2[0], win2[1]), tabs)
    factor = 2.0 - 2.0 * amp[...] * lax.rsqrt(far_re * far_re + far_im * far_im + EPS_AMP)
    back_re, back_im = inverse(factor * far_re, factor * far_im, tabs)
    spread(1, *conj_product(arrive[0], arrive[1], back_re, back_im))
    fsides[1].start()
    spec = forward(*conj_product(win2[0], win2[1], back_re, back_im), tabs)
    ent_re, ent_im = inverse(*conj_product(kern[0], kern[1], *spec), tabs)
    gprobe[0], gprobe[1] = conj_product(win1[0], win1[1], ent_re, ent_im)

    both_cores = remote(gprobe.at[1 - core], recv_a, ar_send.at[0, 0], ar_recv.at[0, 0], partner)
    both_cores.start()
    spread(0, *conj_product(probe[0], probe[1], ent_re, ent_im))
    fsides[0].start()
    both_cores.wait_recv()
    half[...] = gprobe[core] + recv_a[...]

    def scatter(d):
        peer = (plane + d) % planes
        return remote(half.at[pl.ds(pl.multiple_of(peer * share, share), share), :], recv_b.at[d],
                      ar_send.at[1, d], ar_recv.at[1, d], plane_peer(d))

    @pl.loop(1, planes)
    def _(d):
        scatter(d).start()

    pass_on(1)
    pass_on(0)
    mine = pl.ds(pl.multiple_of(plane * share, share), share)
    recv_b[0] = half[mine, :]

    @pl.loop(1, planes)
    def _(d):
        scatter(d).wait_recv()

    total = recv_b[0]
    for d in range(1, planes):
        total = total + recv_b[d]
    sum_b[...] = total

    def across(d):
        return remote(sum_b, recv_c.at[z], ar_send.at[2, d], ar_recv.at[2, d], z_peer(d))

    @pl.loop(1, zs)
    def _(d):
        across(d).start()

    recv_c[z] = total
    collect(1)
    store1 = pltpu.make_async_copy(owned.at[1], obj_out.at[1], out_sem.at[1])
    store1.start()
    @pl.loop(1, zs)
    def _(d):
        across(d).wait_recv()

    total = recv_c[0]
    for d in range(1, zs):
        total = total + recv_c[d]
    final[core, mine, :] = total

    def gather(d):
        return remote(final.at[core, mine, :], final.at[core, mine, :], ar_send.at[3, d], ar_recv.at[3, d], plane_peer(d))

    def hand_over(d):
        owner = (plane - d + planes) % planes
        place = final.at[core, pl.ds(pl.multiple_of(owner * share, share), share), :]
        return remote(place, place, ar_send.at[4, d], ar_recv.at[4, d], partner)

    @pl.loop(1, planes)
    def _(d):
        gather(d).start()

    hand_over(0).start()
    collect(0)
    store0 = pltpu.make_async_copy(owned.at[0], obj_out.at[0], out_sem.at[0])
    store0.start()
    @pl.loop(1, planes)
    def _(d):
        gather(d).wait_recv()
        hand_over(d).start()

    @pl.loop(0, planes)
    def _(d):
        hand_over(d).wait_recv()

    store2 = pltpu.make_async_copy(final, probe_out, out_sem.at[2])
    store2.start()

    for s in (0, 1):
        for copy in [*hops[s], *halo_row[s], sides[s], fsides[s], *fhops[s], *frows[s]]:
            copy.wait_send()
    exchange.wait_send()
    both_cores.wait_send()
    hand_over(0).wait_send()

    @pl.loop(1, planes)
    def _(d):
        scatter(d).wait_send()
        gather(d).wait_send()
        hand_over(d).wait_send()

    @pl.loop(1, zs)
    def _(d):
        across(d).wait_send()

    store0.wait()
    store1.wait()
    store2.wait()


def body(rows, cols, object_field, probe, phase, amplitudes, offsets):
    planes, zs = cols // 2, rows
    share = N // planes
    vmem = lambda *shape: pltpu.VMEM(shape, F32)
    dma = pltpu.SemaphoreType.DMA
    hbm = pl.BlockSpec(memory_space=pl.ANY)
    return pl.pallas_call(
        functools.partial(kernel, rows, cols),
        out_shape=(
            jax.ShapeDtypeStruct((2, 2, N, N), F32),
            jax.ShapeDtypeStruct((2, N, N), F32),
        ),
        in_specs=[hbm, hbm, hbm, hbm, pl.BlockSpec(memory_space=pltpu.SMEM), hbm, hbm],
        out_specs=(hbm, hbm),
        scratch_shapes=[
            vmem(2, 2, EXT, N),
            vmem(2, N, HALF),
            vmem(2, EXT, HALF),
            vmem(2, N, HALF),
            vmem(2, N, HALF),
            vmem(2, N, N),
            vmem(N, N),
            vmem(N, N),
            pltpu.VMEM((4, 2 * N, N), BF16),
            pltpu.VMEM((2, N, N), BF16),
            pltpu.SMEM((1, 1, 1, 2), jnp.int32),
            vmem(2, N, N),
            vmem(2, N, N),
            vmem(2, N, N),
            vmem(2, N, N),
            vmem(2, 2, EXT, N),
            vmem(2, N, HALF),
            vmem(2, N, HALF),
            vmem(2, EXT, HALF),
            vmem(2, 2, 2, MARGIN, N),
            vmem(2, N, HALF),
            vmem(2, 2, MARGIN, HALF),
            vmem(2, N, N),
            vmem(N, N),
            vmem(N, N),
            vmem(planes, share, N),
            vmem(share, N),
            vmem(zs, share, N),
            vmem(2, N, N),
            vmem(2, 2, N, N),
            dma((7,)),
            dma((2,)),
            dma((2, 6)),
            dma((2, 6)),
            dma((2, 6)),
            dma((2, 6)),
            dma((5, 16)),
            dma((5, 16)),
            dma((3,)),
        ],
        compiler_params=pltpu.CompilerParams(
            collective_id=0, has_side_effects=True, vmem_limit_bytes=63 * 1024 * 1024
        ),
    )(object_field, probe, phase, amplitudes, offsets, jnp.asarray(dft_constants()), jnp.asarray(order_constant()))


def solution(mesh):
    placed = (
        P(None, None, "row", "col"),
        P(),
        P(),
        P("row", "col", None, None, None),
        P("row", "col", None, None),
    )
    return jax.shard_map(
        functools.partial(body, mesh.shape["row"], mesh.shape["col"]),
        mesh=mesh,
        in_specs=placed,
        out_specs=(P(None, None, "row", "col"), P()),
        check_vma=False,
    )
```

```python
import functools

import jax
import jax.numpy as jnp
import ml_dtypes
import numpy as np
from jax import lax
from jax.experimental import pallas as pl
from jax.experimental.pallas import tpu as pltpu
from jax.sharding import PartitionSpec as P

EPS_AMP = 0.5
MESH = pl.DeviceIdType.MESH
N = 256
HALF = N // 2
MARGIN = 64
EXT = N + 2 * MARGIN
F32 = jnp.float32
BF16 = jnp.bfloat16


def dft_constants():
    j = np.arange(HALF)[:, None]
    k = np.arange(HALF)[None, :]
    mats = []
    for odd in (0, 1):
        angle = -2.0 * np.pi * (((2 * j + odd) * k) % N) / N
        re, im = np.cos(angle) / 16.0, np.sin(angle) / 16.0
        mats.append(np.block([[re, -im], [im, re]]))
    mats += [mats[0].T, mats[1].T]
    out = []
    for m in mats:
        hi = m.astype(ml_dtypes.bfloat16)
        lo = (m - hi.astype(np.float64)).astype(ml_dtypes.bfloat16)
        out.append(np.concatenate([hi, lo], axis=0))
    return np.stack(out)


def order_constant():
    q = np.zeros((N, N), np.float32)
    q[np.arange(HALF), 2 * np.arange(HALF)] = 1.0
    q[HALF + np.arange(HALF), 2 * np.arange(HALF) + 1] = 1.0
    return np.stack([q, q.T]).astype(ml_dtypes.bfloat16)


def dot(a, b):
    return jnp.dot(a, b, preferred_element_type=F32)


def two_terms(x):
    hi = x.astype(BF16)
    return hi, (x - hi.astype(F32)).astype(BF16)


def left_apply(table, x):
    hi, lo = two_terms(x)
    both = dot(table[...], hi)
    return both[:N] + both[N:] + dot(table[:N], lo)


def right_apply(x, table):
    hi, lo = two_terms(x)
    return dot(hi, table[:N]) + dot(lo, table[:N]) + dot(hi, table[N:])


def left_forward(x_re, x_im, tabs):
    low = jnp.concatenate([x_re[:HALF], x_im[:HALF]], axis=0)
    high = jnp.concatenate([x_re[HALF:], x_im[HALF:]], axis=0)
    even = left_apply(tabs.at[0], low + high)
    odd = left_apply(tabs.at[1], low - high)
    return (
        jnp.concatenate([even[:HALF], odd[:HALF]], axis=0),
        jnp.concatenate([even[HALF:], odd[HALF:]], axis=0),
    )


def right_forward(x_re, x_im, tabs):
    low = jnp.concatenate([x_re[:, :HALF], x_im[:, :HALF]], axis=1)
    high = jnp.concatenate([x_re[:, HALF:], x_im[:, HALF:]], axis=1)
    even = right_apply(low + high, tabs.at[2])
    odd = right_apply(low - high, tabs.at[3])
    return (
        jnp.concatenate([even[:, :HALF], odd[:, :HALF]], axis=1),
        jnp.concatenate([even[:, HALF:], odd[:, HALF:]], axis=1),
    )


def left_inverse(x_re, x_im, tabs):
    a = left_apply(tabs.at[2], jnp.concatenate([x_re[:HALF], x_im[:HALF]], axis=0))
    b = left_apply(tabs.at[3], jnp.concatenate([x_re[HALF:], x_im[HALF:]], axis=0))
    low, high = a + b, a - b
    return (
        jnp.concatenate([low[:HALF], high[:HALF]], axis=0),
        jnp.concatenate([low[HALF:], high[HALF:]], axis=0),
    )


def right_inverse(x_re, x_im, tabs):
    a = right_apply(jnp.concatenate([x_re[:, :HALF], x_im[:, :HALF]], axis=1), tabs.at[0])
    b = right_apply(jnp.concatenate([x_re[:, HALF:], x_im[:, HALF:]], axis=1), tabs.at[1])
    low, high = a + b, a - b
    return (
        jnp.concatenate([low[:, :HALF], high[:, :HALF]], axis=1),
        jnp.concatenate([low[:, HALF:], high[:, HALF:]], axis=1),
    )


def forward(x_re, x_im, tabs):
    return right_forward(*left_forward(x_re, x_im, tabs), tabs)


def inverse(x_re, x_im, tabs):
    return right_inverse(*left_inverse(x_re, x_im, tabs), tabs)


def product(a_re, a_im, b_re, b_im):
    return a_re * b_re - a_im * b_im, a_re * b_im + a_im * b_re


def conj_product(a_re, a_im, b_re, b_im):
    return a_re * b_re + a_im * b_im, a_re * b_im - a_im * b_re


def reorder(x, order):
    hi = x.astype(BF16)
    rest = x - hi.astype(F32)
    mid = rest.astype(BF16)
    low = (rest - mid.astype(F32)).astype(BF16)
    parts = []
    for term in (hi, mid, low):
        rows = dot(order[0], term).astype(BF16)
        parts.append(dot(rows, order[1]))
    return parts[0] + parts[1] + parts[2]


def cos_sin(x):
    h = 0.5 * x
    t = h * h
    s = h * (1.0 + t * (-1.0 / 6 + t * (1.0 / 120 + t * (-1.0 / 5040 + t * (
        1.0 / 362880 + t * (-1.0 / 39916800 + t * (1.0 / 6227020800)))))))
    c = 1.0 + t * (-0.5 + t * (1.0 / 24 + t * (-1.0 / 720 + t * (1.0 / 40320 + t * (
        -1.0 / 3628800 + t * (1.0 / 479001600 + t * (-1.0 / 87178291200)))))))
    return 1.0 - 2.0 * s * s, 2.0 * s * c


def kernel(
    rows, cols,
    obj, probe_in, phase_in, amp_in, offs, tabs_in, order_in,
    obj_out, probe_out,
    mid, pack, hop, pick, side, probe, phase, amp, tabs, order, peer_offs, win1, win2, arrive, kern,
    gmid, gpick, gside, ghop, rrow, rhop, rcor, gprobe, recv_a, half, recv_b, sum_b, recv_c, final, owned,
    in_sem, offs_sem, halo_send, halo_recv, fold_send, fold_recv, ar_send, ar_recv, out_sem,
):
    row, col = lax.axis_index("row"), lax.axis_index("col")
    core, z_hi = row % 2, row // 2
    plane, z_lo = col // 2, col % 2
    planes, zs = cols // 2, rows
    z = z_hi * 2 + z_lo
    share = N // planes

    def neighbour(dr, dc):
        return ((row + dr + rows) % rows, (col + dc + cols) % cols)

    hop_to = 4 * z_lo - 2
    pair_peer = (row, col + 1 - 2 * z_lo)
    partner = (z_hi * 2 + 1 - core, col)

    def plane_peer(d):
        return (row, ((plane + d) % planes) * 2 + z_lo)

    def z_peer(d):
        other = (z + d) % zs
        return ((other // 2) * 2 + core, plane * 2 + other % 2)

    loads = [
        pltpu.make_async_copy(obj.at[0], mid.at[0, :, pl.ds(MARGIN, N), :], in_sem.at[0]),
        pltpu.make_async_copy(obj.at[1], mid.at[1, :, pl.ds(MARGIN, N), :], in_sem.at[1]),
        pltpu.make_async_copy(probe_in, probe, in_sem.at[2]),
        pltpu.make_async_copy(phase_in, phase, in_sem.at[3]),
        pltpu.make_async_copy(order_in, order, in_sem.at[4]),
        pltpu.make_async_copy(amp_in.at[0, 0, 0], amp, in_sem.at[5]),
        pltpu.make_async_copy(tabs_in, tabs, in_sem.at[6]),
    ]
    for load in loads:
        load.start()

    barrier = pltpu.get_barrier_semaphore()
    for step in ((-1, 0), (1, 0), (-1, -2), (-1, 2), (1, -2), (1, 2)):
        pl.semaphore_signal(barrier, inc=1, device_id=neighbour(*step), device_id_type=MESH)

    @pl.loop(1, planes)
    def _(d):
        pl.semaphore_signal(barrier, inc=1, device_id=plane_peer(d), device_id_type=MESH)

    @pl.loop(1, zs)
    def _(d):
        pl.semaphore_signal(barrier, inc=1, device_id=z_peer(d), device_id_type=MESH)

    lane = lax.broadcasted_iota(jnp.int32, (N, HALF), 1)
    lower = lax.broadcasted_iota(jnp.int32, (EXT, HALF), 1) < 64

    def left_margin(re, im):
        return jnp.where(lower[:re.shape[0]], re, pltpu.roll(im, 64, 1))

    def right_margin(re, im):
        return jnp.where(lower[:re.shape[0]], pltpu.roll(re, 64, 1), im)

    def pack_outer(s):
        inner = pl.ds(MARGIN, N)

        @pl.when(z_lo == 0)
        def _():
            pack[s] = left_margin(mid[s, 0, inner, :HALF], mid[s, 1, inner, :HALF])

        @pl.when(z_lo == 1)
        def _():
            pack[s] = right_margin(mid[s, 0, inner, HALF:], mid[s, 1, inner, HALF:])

    def remote(src, dst, send, recv, device):
        return pltpu.make_async_remote_copy(
            src_ref=src, dst_ref=dst, send_sem=send, recv_sem=recv, device_id=device, device_id_type=MESH)

    top, inner, bottom = pl.ds(0, MARGIN), pl.ds(MARGIN, N), pl.ds(MARGIN + N, MARGIN)

    def halo_hops(s):
        moves = (
            (pack.at[s], hop.at[s, inner, :], (0, hop_to)),
            (pack.at[s, pl.ds(0, MARGIN), :], hop.at[s, bottom, :], (-1, hop_to)),
            (pack.at[s, pl.ds(N - MARGIN, MARGIN), :], hop.at[s, top, :], (1, hop_to)),
        )
        return [remote(src, dst, halo_send.at[s, i], halo_recv.at[s, i], neighbour(*step))
                for i, (src, dst, step) in enumerate(moves)]

    def halo_rows(s):
        moves = (
            (mid.at[s, :, pl.ds(MARGIN, MARGIN), :], mid.at[s, :, bottom, :], (-1, 0)),
            (mid.at[s, :, pl.ds(N, MARGIN), :], mid.at[s, :, top, :], (1, 0)),
        )
        return [remote(src, dst, halo_send.at[s, 3 + i], halo_recv.at[s, 3 + i], neighbour(*step))
                for i, (src, dst, step) in enumerate(moves)]

    def halo_side(s):
        return remote(pick.at[s], side.at[s], halo_send.at[s, 5], halo_recv.at[s, 5], pair_peer)

    hops, halo_row, sides = ([f(s) for s in (0, 1)] for f in (halo_hops, halo_rows, halo_side))
    exchange = remote(offs, peer_offs, offs_sem.at[0], offs_sem.at[1], pair_peer)
    loads[0].wait()
    pack_outer(0)
    pl.semaphore_wait(barrier, 6 + planes - 1 + zs - 1)
    exchange.start()
    for copy in halo_row[0] + hops[0]:
        copy.start()
    loads[1].wait()
    pack_outer(1)
    for copy in halo_row[1] + hops[1]:
        copy.start()

    loads[3].wait()
    loads[4].wait()
    kern[0], kern[1] = cos_sin(reorder(phase[...], order))
    loads[5].wait()
    amp[...] = reorder(amp[...], order)
    loads[2].wait()
    loads[6].wait()

    off_y, off_x = offs[0, 0, 0, 0], offs[0, 0, 0, 1]
    shift = off_x - MARGIN

    outside = jnp.logical_or(
        jnp.logical_and(col == 0, off_x < MARGIN), jnp.logical_and(col == cols - 1, off_x > MARGIN))
    inside = 1.0 - outside.astype(F32)

    def clear_edges(s):
        @pl.when(row == 0)
        def _():
            mid[s, :, top, :] = jnp.zeros((2, MARGIN, N), F32)
            hop[s, top, :] = jnp.zeros((MARGIN, HALF), F32)

        @pl.when(row == rows - 1)
        def _():
            mid[s, :, bottom, :] = jnp.zeros((2, MARGIN, N), F32)
            hop[s, bottom, :] = jnp.zeros((MARGIN, HALF), F32)

    def up(x, amount):
        return pltpu.roll(x, lax.rem(EXT - amount, EXT), 0)[:N]

    def down(x, amount):
        below = jnp.zeros((EXT - N, x.shape[1]), F32)
        return pltpu.roll(jnp.concatenate([x, below], axis=0), amount, 0)

    def peer_takes_own(shape):
        reach = (peer_offs[0, 0, 0, 1] - MARGIN) * (1 - 2 * z_lo)
        return lax.broadcasted_iota(jnp.int32, shape, 1) * 0 + reach < 0

    def choose(s):
        own = peer_takes_own((EXT, HALF))

        @pl.when(z_lo == 0)
        def _():
            mine = right_margin(mid[s, 0, :, HALF:], mid[s, 1, :, HALF:])
            pick[s] = up(jnp.where(own, mine, hop[s]), peer_offs[0, 0, 0, 0])

        @pl.when(z_lo == 1)
        def _():
            mine = left_margin(mid[s, 0, :, :HALF], mid[s, 1, :, :HALF])
            pick[s] = up(jnp.where(own, mine, hop[s]), peer_offs[0, 0, 0, 0])

    over_right, over_left = lane < shift, lane >= HALF + shift

    def window(s, ref):
        beside = side[s] * inside
        turned = pltpu.roll(beside, 64, 1)
        for part in (0, 1):
            both = up(mid[s, part], off_y)
            low = jnp.where(over_right, beside if part == 0 else turned, both[:, :HALF])
            high = jnp.where(over_left, turned if part == 0 else beside, both[:, HALF:])
            ref[part] = pltpu.roll(jnp.concatenate([low, high], axis=1), lax.rem(N + MARGIN - off_x, N), 1)

    def spread(s, g_re, g_im):
        zero = jnp.zeros((N, HALF), F32)
        lefts, rights = [], []
        for part, g in ((0, g_re), (1, g_im)):
            moved = pltpu.roll(g, lax.rem(off_x + N - MARGIN, N), 1)
            low, high = moved[:, :HALF], moved[:, HALF:]
            rights.append(jnp.where(over_right, low, zero))
            lefts.append(jnp.where(over_left, high, zero))
            kept = [jnp.where(over_right, zero, low), jnp.where(over_left, zero, high)]
            gmid[s, part] = down(jnp.concatenate(kept, axis=1), off_y)
        gpick[s] = right_margin(*lefts) + left_margin(*rights)

    def fold_side(s):
        return remote(gpick.at[s], gside.at[s], fold_send.at[s, 5], fold_recv.at[s, 5], pair_peer)

    def fold_hops(s):
        moves = (
            (ghop.at[s, inner, :], rhop.at[s], (0, -hop_to)),
            (ghop.at[s, top, :], rcor.at[s, 0], (-1, -hop_to)),
            (ghop.at[s, bottom, :], rcor.at[s, 1], (1, -hop_to)),
        )
        return [remote(src, dst, fold_send.at[s, i], fold_recv.at[s, i], neighbour(*step))
                for i, (src, dst, step) in enumerate(moves)]

    def fold_rows(s):
        moves = (
            (gmid.at[s, :, top, :], rrow.at[s, 0], (-1, 0)),
            (gmid.at[s, :, bottom, :], rrow.at[s, 1], (1, 0)),
        )
        return [remote(src, dst, fold_send.at[s, 3 + i], fold_recv.at[s, 3 + i], neighbour(*step))
                for i, (src, dst, step) in enumerate(moves)]

    fsides, fhops, frows = ([f(s) for s in (0, 1)] for f in (fold_side, fold_hops, fold_rows))

    def add_packed(ref, s, place, packed, lefthand):
        low = lower[:packed.shape[0]]
        turned = pltpu.roll(packed, 64, 1)
        if lefthand:
            ref[s, 0, place, :HALF] += jnp.where(low, packed, 0.0)
            ref[s, 1, place, :HALF] += jnp.where(low, turned, 0.0)
        else:
            ref[s, 0, place, HALF:] += jnp.where(low, 0.0, turned)
            ref[s, 1, place, HALF:] += jnp.where(low, 0.0, packed)

    def pass_on(s):
        fsides[s].wait_recv()
        got = down(gside[s], peer_offs[0, 0, 0, 0])
        own = peer_takes_own((EXT, HALF))
        ghop[s] = jnp.where(own, 0.0, got)
        for copy in fhops[s]:
            copy.start()
        here = jnp.where(own, got, 0.0)

        @pl.when(z_lo == 0)
        def _():
            add_packed(gmid, s, pl.ds(0, EXT), here, False)

        @pl.when(z_lo == 1)
        def _():
            add_packed(gmid, s, pl.ds(0, EXT), here, True)

        for copy in frows[s]:
            copy.start()

    first, last = pl.ds(0, MARGIN), pl.ds(N - MARGIN, MARGIN)

    def collect(s):
        for copy in fhops[s] + frows[s]:
            copy.wait_recv()
        for part in (0, 1):
            owned[s, part] = gmid[s, part, inner, :]

        @pl.when(row < rows - 1)
        def _():
            owned[s, :, last, :] += rrow[s, 0]

        @pl.when(row > 0)
        def _():
            owned[s, :, first, :] += rrow[s, 1]

        for lo, valid in ((0, col > 0), (1, col < cols - 1)):
            @pl.when(jnp.logical_and(z_lo == lo, valid))
            def _():
                add_packed(owned, s, pl.ds(0, N), rhop[s], lo == 0)

                @pl.when(row < rows - 1)
                def _():
                    add_packed(owned, s, last, rcor[s, 0], lo == 0)

                @pl.when(row > 0)
                def _():
                    add_packed(owned, s, first, rcor[s, 1], lo == 0)

    exchange.wait_recv()
    for copy in halo_row[0] + hops[0]:
        copy.wait_recv()
    clear_edges(0)
    choose(0)
    sides[0].start()
    for copy in halo_row[1] + hops[1]:
        copy.wait_recv()
    clear_edges(1)
    choose(1)
    sides[1].start()
    sides[0].wait_recv()
    window(0, win1)
    entry = product(probe[0], probe[1], win1[0], win1[1])
    spectrum = forward(*entry, tabs)
    moved = product(kern[0], kern[1], *spectrum)
    arrive[0], arrive[1] = inverse(*moved, tabs)

    sides[1].wait_recv()
    window(1, win2)
    far_re, far_im = forward(*product(arrive[0], arrive[1], win2[0], win2[1]), tabs)
    factor = 2.0 - 2.0 * amp[...] * lax.rsqrt(far_re * far_re + far_im * far_im + EPS_AMP)
    back_re, back_im = inverse(factor * far_re, factor * far_im, tabs)
    spread(1, *conj_product(arrive[0], arrive[1], back_re, back_im))
    fsides[1].start()
    spec = forward(*conj_product(win2[0], win2[1], back_re, back_im), tabs)
    ent_re, ent_im = inverse(*conj_product(kern[0], kern[1], *spec), tabs)
    gprobe[0], gprobe[1] = conj_product(win1[0], win1[1], ent_re, ent_im)

    both_cores = remote(gprobe.at[1 - core], recv_a, ar_send.at[0, 0], ar_recv.at[0, 0], partner)
    both_cores.start()
    spread(0, *conj_product(probe[0], probe[1], ent_re, ent_im))
    fsides[0].start()
    both_cores.wait_recv()
    half[...] = gprobe[core] + recv_a[...]

    def scatter(d):
        peer = (plane + d) % planes
        return remote(half.at[pl.ds(pl.multiple_of(peer * share, share), share), :], recv_b.at[d],
                      ar_send.at[1, d], ar_recv.at[1, d], plane_peer(d))

    @pl.loop(1, planes)
    def _(d):
        scatter(d).start()

    pass_on(1)
    mine = pl.ds(pl.multiple_of(plane * share, share), share)
    recv_b[0] = half[mine, :]

    @pl.loop(1, planes)
    def _(d):
        scatter(d).wait_recv()

    total = recv_b[0]
    for d in range(1, planes):
        total = total + recv_b[d]
    sum_b[...] = total

    def across(d):
        return remote(sum_b, recv_c.at[z], ar_send.at[2, d], ar_recv.at[2, d], z_peer(d))

    @pl.loop(1, zs)
    def _(d):
        across(d).start()

    recv_c[z] = total
    @pl.loop(1, zs)
    def _(d):
        across(d).wait_recv()

    total = recv_c[0]
    for d in range(1, zs):
        total = total + recv_c[d]
    final[core, mine, :] = total

    def gather(d):
        return remote(final.at[core, mine, :], final.at[core, mine, :], ar_send.at[3, d], ar_recv.at[3, d], plane_peer(d))

    def hand_over(d):
        owner = (plane - d + planes) % planes
        place = final.at[core, pl.ds(pl.multiple_of(owner * share, share), share), :]
        return remote(place, place, ar_send.at[4, d], ar_recv.at[4, d], partner)

    @pl.loop(1, planes)
    def _(d):
        gather(d).start()

    hand_over(0).start()
    pass_on(0)
    collect(1)
    store1 = pltpu.make_async_copy(owned.at[1], obj_out.at[1], out_sem.at[1])
    store1.start()
    @pl.loop(1, planes)
    def _(d):
        gather(d).wait_recv()
        hand_over(d).start()

    collect(0)
    store0 = pltpu.make_async_copy(owned.at[0], obj_out.at[0], out_sem.at[0])
    store0.start()
    @pl.loop(0, planes)
    def _(d):
        hand_over(d).wait_recv()

    store2 = pltpu.make_async_copy(final, probe_out, out_sem.at[2])
    store2.start()

    for s in (0, 1):
        for copy in [*hops[s], *halo_row[s], sides[s], fsides[s], *fhops[s], *frows[s]]:
            copy.wait_send()
    exchange.wait_send()
    both_cores.wait_send()
    hand_over(0).wait_send()

    @pl.loop(1, planes)
    def _(d):
        scatter(d).wait_send()
        gather(d).wait_send()
        hand_over(d).wait_send()

    @pl.loop(1, zs)
    def _(d):
        across(d).wait_send()

    store0.wait()
    store1.wait()
    store2.wait()


def body(rows, cols, object_field, probe, phase, amplitudes, offsets):
    planes, zs = cols // 2, rows
    share = N // planes
    vmem = lambda *shape: pltpu.VMEM(shape, F32)
    dma = pltpu.SemaphoreType.DMA
    hbm = pl.BlockSpec(memory_space=pl.ANY)
    return pl.pallas_call(
        functools.partial(kernel, rows, cols),
        out_shape=(
            jax.ShapeDtypeStruct((2, 2, N, N), F32),
            jax.ShapeDtypeStruct((2, N, N), F32),
        ),
        in_specs=[hbm, hbm, hbm, hbm, pl.BlockSpec(memory_space=pltpu.SMEM), hbm, hbm],
        out_specs=(hbm, hbm),
        scratch_shapes=[
            vmem(2, 2, EXT, N),
            vmem(2, N, HALF),
            vmem(2, EXT, HALF),
            vmem(2, N, HALF),
            vmem(2, N, HALF),
            vmem(2, N, N),
            vmem(N, N),
            vmem(N, N),
            pltpu.VMEM((4, 2 * N, N), BF16),
            pltpu.VMEM((2, N, N), BF16),
            pltpu.SMEM((1, 1, 1, 2), jnp.int32),
            vmem(2, N, N),
            vmem(2, N, N),
            vmem(2, N, N),
            vmem(2, N, N),
            vmem(2, 2, EXT, N),
            vmem(2, N, HALF),
            vmem(2, N, HALF),
            vmem(2, EXT, HALF),
            vmem(2, 2, 2, MARGIN, N),
            vmem(2, N, HALF),
            vmem(2, 2, MARGIN, HALF),
            vmem(2, N, N),
            vmem(N, N),
            vmem(N, N),
            vmem(planes, share, N),
            vmem(share, N),
            vmem(zs, share, N),
            vmem(2, N, N),
            vmem(2, 2, N, N),
            dma((7,)),
            dma((2,)),
            dma((2, 6)),
            dma((2, 6)),
            dma((2, 6)),
            dma((2, 6)),
            dma((5, 16)),
            dma((5, 16)),
            dma((3,)),
        ],
        compiler_params=pltpu.CompilerParams(
            collective_id=0, has_side_effects=True, vmem_limit_bytes=63 * 1024 * 1024
        ),
    )(object_field, probe, phase, amplitudes, offsets, jnp.asarray(dft_constants()), jnp.asarray(order_constant()))


def solution(mesh):
    placed = (
        P(None, None, "row", "col"),
        P(),
        P(),
        P("row", "col", None, None, None),
        P("row", "col", None, None),
    )
    return jax.shard_map(
        functools.partial(body, mesh.shape["row"], mesh.shape["col"]),
        mesh=mesh,
        in_specs=placed,
        out_specs=(P(None, None, "row", "col"), P()),
        check_vma=False,
    )
```

```python
import functools
import math

import jax
import jax.numpy as jnp
import ml_dtypes
import numpy as np
from jax import lax
from jax.experimental import pallas as pl
from jax.experimental.pallas import tpu as pltpu
from jax.sharding import PartitionSpec as P

EPS_AMP = 0.5
MESH = pl.DeviceIdType.MESH
N = 256
HALF = N // 2
MARGIN = 64
EXT = N + 2 * MARGIN
F32 = jnp.float32
BF16 = jnp.bfloat16


def dft_constants():
    j = np.arange(HALF)[:, None]
    k = np.arange(HALF)[None, :]
    mats = []
    for odd in (0, 1):
        angle = -2.0 * np.pi * (((2 * j + odd) * k) % N) / N
        re, im = np.cos(angle) / 16.0, np.sin(angle) / 16.0
        mats.append(np.block([[re, -im], [im, re]]))
    mats += [mats[0].T, mats[1].T]
    out = []
    for m in mats:
        hi = m.astype(ml_dtypes.bfloat16)
        lo = (m - hi.astype(np.float64)).astype(ml_dtypes.bfloat16)
        out.append(np.concatenate([hi, lo], axis=0))
    return np.stack(out)


def order_constant():
    q = np.zeros((N, N), np.float32)
    q[np.arange(HALF), 2 * np.arange(HALF)] = 1.0
    q[HALF + np.arange(HALF), 2 * np.arange(HALF) + 1] = 1.0
    return np.stack([q, q.T]).astype(ml_dtypes.bfloat16)


def dot(a, b):
    return jnp.dot(a, b, preferred_element_type=F32)


def two_terms(x):
    hi = x.astype(BF16)
    return hi, (x - hi.astype(F32)).astype(BF16)


def left_apply(table, x):
    hi, lo = two_terms(x)
    both = dot(table[...], hi)
    return both[:N] + both[N:] + dot(table[:N], lo)


def right_apply(x, table):
    hi, lo = two_terms(x)
    return dot(hi, table[:N]) + dot(lo, table[:N]) + dot(hi, table[N:])


def left_forward(x_re, x_im, tabs):
    low = jnp.concatenate([x_re[:HALF], x_im[:HALF]], axis=0)
    high = jnp.concatenate([x_re[HALF:], x_im[HALF:]], axis=0)
    even = left_apply(tabs.at[0], low + high)
    odd = left_apply(tabs.at[1], low - high)
    return (
        jnp.concatenate([even[:HALF], odd[:HALF]], axis=0),
        jnp.concatenate([even[HALF:], odd[HALF:]], axis=0),
    )


def right_forward(x_re, x_im, tabs):
    low = jnp.concatenate([x_re[:, :HALF], x_im[:, :HALF]], axis=1)
    high = jnp.concatenate([x_re[:, HALF:], x_im[:, HALF:]], axis=1)
    even = right_apply(low + high, tabs.at[2])
    odd = right_apply(low - high, tabs.at[3])
    return (
        jnp.concatenate([even[:, :HALF], odd[:, :HALF]], axis=1),
        jnp.concatenate([even[:, HALF:], odd[:, HALF:]], axis=1),
    )


def left_inverse(x_re, x_im, tabs):
    a = left_apply(tabs.at[2], jnp.concatenate([x_re[:HALF], x_im[:HALF]], axis=0))
    b = left_apply(tabs.at[3], jnp.concatenate([x_re[HALF:], x_im[HALF:]], axis=0))
    low, high = a + b, a - b
    return (
        jnp.concatenate([low[:HALF], high[:HALF]], axis=0),
        jnp.concatenate([low[HALF:], high[HALF:]], axis=0),
    )


def right_inverse(x_re, x_im, tabs):
    a = right_apply(jnp.concatenate([x_re[:, :HALF], x_im[:, :HALF]], axis=1), tabs.at[0])
    b = right_apply(jnp.concatenate([x_re[:, HALF:], x_im[:, HALF:]], axis=1), tabs.at[1])
    low, high = a + b, a - b
    return (
        jnp.concatenate([low[:, :HALF], high[:, :HALF]], axis=1),
        jnp.concatenate([low[:, HALF:], high[:, HALF:]], axis=1),
    )


def forward(x_re, x_im, tabs):
    return right_forward(*left_forward(x_re, x_im, tabs), tabs)


def inverse(x_re, x_im, tabs):
    return right_inverse(*left_inverse(x_re, x_im, tabs), tabs)


def product(a_re, a_im, b_re, b_im):
    return a_re * b_re - a_im * b_im, a_re * b_im + a_im * b_re


def conj_product(a_re, a_im, b_re, b_im):
    return a_re * b_re + a_im * b_im, a_re * b_im - a_im * b_re


def reorder(x, order):
    hi = x.astype(BF16)
    rest = x - hi.astype(F32)
    mid = rest.astype(BF16)
    low = (rest - mid.astype(F32)).astype(BF16)
    parts = []
    for term in (hi, mid, low):
        rows = dot(order[0], term).astype(BF16)
        parts.append(dot(rows, order[1]))
    return parts[0] + parts[1] + parts[2]


def cos_sin(x):
    h = 0.5 * x
    t = h * h
    s = h * (1.0 + t * (-1.0 / 6 + t * (1.0 / 120 + t * (-1.0 / 5040 + t * (
        1.0 / 362880 + t * (-1.0 / 39916800 + t * (1.0 / 6227020800)))))))
    c = 1.0 + t * (-0.5 + t * (1.0 / 24 + t * (-1.0 / 720 + t * (1.0 / 40320 + t * (
        -1.0 / 3628800 + t * (1.0 / 479001600 + t * (-1.0 / 87178291200)))))))
    return 1.0 - 2.0 * s * s, 2.0 * s * c


def kernel(
    rows, cols,
    obj, probe_in, phase_in, amp_in, offs, tabs_in, order_in,
    obj_out, probe_out,
    mid, pack, hop, pick, side, probe, phase, amp, tabs, order, peer_offs, win1, win2, arrive, kern,
    gmid, gpick, gside, ghop, rrow, rhop, rcor, gprobe, recv_a, half, recv_b, sum_b, recv_c, final, owned,
    in_sem, offs_sem, halo_send, halo_recv, fold_send, fold_recv, ar_send, ar_recv, out_sem,
):
    row, col = lax.axis_index("row"), lax.axis_index("col")
    core, z_hi = row % 2, row // 2
    plane, z_lo = col // 2, col % 2
    planes, zs = cols // 2, rows
    z = z_hi * 2 + z_lo
    share = N // planes

    def neighbour(dr, dc):
        return ((row + dr + rows) % rows, (col + dc + cols) % cols)

    hop_to = 4 * z_lo - 2
    pair_peer = (row, col + 1 - 2 * z_lo)
    partner = (z_hi * 2 + 1 - core, col)

    side_len = math.isqrt(planes)
    far = lambda step, length: min(step, length - step)
    plane_steps = sorted(
        range(1, planes), key=lambda k: -far(k // side_len, side_len) - far(k % side_len, side_len))
    z_steps = sorted(range(1, zs), key=lambda k: -far(k, zs))

    def plane_at(k, sign=1):
        x, y = plane // side_len, plane % side_len
        return (x + side_len + sign * (k // side_len)) % side_len * side_len + (y + side_len + sign * (k % side_len)) % side_len

    def plane_peer(k):
        return (row, plane_at(k) * 2 + z_lo)

    def z_peer(k):
        other = (z + k) % zs
        return ((other // 2) * 2 + core, plane * 2 + other % 2)

    barrier = pltpu.get_barrier_semaphore()
    for step in ((-1, 0), (1, 0), (-1, -2), (-1, 2), (1, -2), (1, 2)):
        pl.semaphore_signal(barrier, inc=1, device_id=neighbour(*step), device_id_type=MESH)

    for k in plane_steps:
        pl.semaphore_signal(barrier, inc=1, device_id=plane_peer(k), device_id_type=MESH)
    for k in z_steps:
        pl.semaphore_signal(barrier, inc=1, device_id=z_peer(k), device_id_type=MESH)

    loads = [
        pltpu.make_async_copy(obj.at[0], mid.at[0, :, pl.ds(MARGIN, N), :], in_sem.at[0]),
        pltpu.make_async_copy(obj.at[1], mid.at[1, :, pl.ds(MARGIN, N), :], in_sem.at[1]),
        pltpu.make_async_copy(probe_in, probe, in_sem.at[2]),
        pltpu.make_async_copy(phase_in, phase, in_sem.at[3]),
        pltpu.make_async_copy(order_in, order, in_sem.at[4]),
        pltpu.make_async_copy(amp_in.at[0, 0, 0], amp, in_sem.at[5]),
        pltpu.make_async_copy(tabs_in, tabs, in_sem.at[6]),
    ]
    for load in loads:
        load.start()

    lane = lax.broadcasted_iota(jnp.int32, (N, HALF), 1)
    lower = lax.broadcasted_iota(jnp.int32, (EXT, HALF), 1) < 64

    def left_margin(re, im):
        return jnp.where(lower[:re.shape[0]], re, pltpu.roll(im, 64, 1))

    def right_margin(re, im):
        return jnp.where(lower[:re.shape[0]], pltpu.roll(re, 64, 1), im)

    def pack_outer(s):
        inner = pl.ds(MARGIN, N)

        @pl.when(z_lo == 0)
        def _():
            pack[s] = left_margin(mid[s, 0, inner, :HALF], mid[s, 1, inner, :HALF])

        @pl.when(z_lo == 1)
        def _():
            pack[s] = right_margin(mid[s, 0, inner, HALF:], mid[s, 1, inner, HALF:])

    def remote(src, dst, send, recv, device):
        return pltpu.make_async_remote_copy(
            src_ref=src, dst_ref=dst, send_sem=send, recv_sem=recv, device_id=device, device_id_type=MESH)

    top, inner, bottom = pl.ds(0, MARGIN), pl.ds(MARGIN, N), pl.ds(MARGIN + N, MARGIN)

    def halo_hops(s):
        moves = (
            (pack.at[s], hop.at[s, inner, :], (0, hop_to)),
            (pack.at[s, pl.ds(0, MARGIN), :], hop.at[s, bottom, :], (-1, hop_to)),
            (pack.at[s, pl.ds(N - MARGIN, MARGIN), :], hop.at[s, top, :], (1, hop_to)),
        )
        return [remote(src, dst, halo_send.at[s, i], halo_recv.at[s, i], neighbour(*step))
                for i, (src, dst, step) in enumerate(moves)]

    def halo_rows(s):
        moves = (
            (obj.at[s, :, pl.ds(0, MARGIN), :], mid.at[s, :, bottom, :], (-1, 0)),
            (obj.at[s, :, pl.ds(N - MARGIN, MARGIN), :], mid.at[s, :, top, :], (1, 0)),
        )
        return [remote(src, dst, halo_send.at[s, 3 + i], halo_recv.at[s, 3 + i], neighbour(*step))
                for i, (src, dst, step) in enumerate(moves)]

    def halo_side(s):
        return remote(pick.at[s], side.at[s], halo_send.at[s, 5], halo_recv.at[s, 5], pair_peer)

    hops, halo_row, sides = ([f(s) for s in (0, 1)] for f in (halo_hops, halo_rows, halo_side))
    exchange = remote(offs, peer_offs, offs_sem.at[0], offs_sem.at[1], pair_peer)
    pl.semaphore_wait(barrier, 6 + planes - 1 + zs - 1)
    for copy in halo_row[0]:
        copy.start()
    exchange.start()
    loads[0].wait()
    pack_outer(0)
    for copy in hops[0]:
        copy.start()
    loads[1].wait()
    pack_outer(1)
    loads[3].wait()
    loads[4].wait()
    kern[0], kern[1] = cos_sin(reorder(phase[...], order))
    loads[5].wait()
    amp[...] = reorder(amp[...], order)
    loads[2].wait()
    loads[6].wait()

    for copy in halo_row[0]:
        copy.wait_send()
    for copy in halo_row[1] + hops[1]:
        copy.start()
    off_y, off_x = offs[0, 0, 0, 0], offs[0, 0, 0, 1]
    shift = off_x - MARGIN

    outside = jnp.logical_or(
        jnp.logical_and(col == 0, off_x < MARGIN), jnp.logical_and(col == cols - 1, off_x > MARGIN))
    inside = 1.0 - outside.astype(F32)

    def clear_edges(s):
        @pl.when(row == 0)
        def _():
            mid[s, :, top, :] = jnp.zeros((2, MARGIN, N), F32)
            hop[s, top, :] = jnp.zeros((MARGIN, HALF), F32)

        @pl.when(row == rows - 1)
        def _():
            mid[s, :, bottom, :] = jnp.zeros((2, MARGIN, N), F32)
            hop[s, bottom, :] = jnp.zeros((MARGIN, HALF), F32)

    def up(x, amount):
        return pltpu.roll(x, lax.rem(EXT - amount, EXT), 0)[:N]

    def down(x, amount):
        below = jnp.zeros((EXT - N, x.shape[1]), F32)
        return pltpu.roll(jnp.concatenate([x, below], axis=0), amount, 0)

    def peer_takes_own(shape):
        reach = (peer_offs[0, 0, 0, 1] - MARGIN) * (1 - 2 * z_lo)
        return lax.broadcasted_iota(jnp.int32, shape, 1) * 0 + reach < 0

    def choose(s):
        own = peer_takes_own((EXT, HALF))

        @pl.when(z_lo == 0)
        def _():
            mine = right_margin(mid[s, 0, :, HALF:], mid[s, 1, :, HALF:])
            pick[s] = up(jnp.where(own, mine, hop[s]), peer_offs[0, 0, 0, 0])

        @pl.when(z_lo == 1)
        def _():
            mine = left_margin(mid[s, 0, :, :HALF], mid[s, 1, :, :HALF])
            pick[s] = up(jnp.where(own, mine, hop[s]), peer_offs[0, 0, 0, 0])

    over_right, over_left = lane < shift, lane >= HALF + shift

    def window(s, ref):
        beside = side[s] * inside
        turned = pltpu.roll(beside, 64, 1)
        for part in (0, 1):
            both = up(mid[s, part], off_y)
            low = jnp.where(over_right, beside if part == 0 else turned, both[:, :HALF])
            high = jnp.where(over_left, turned if part == 0 else beside, both[:, HALF:])
            ref[part] = pltpu.roll(jnp.concatenate([low, high], axis=1), lax.rem(N + MARGIN - off_x, N), 1)

    def spread(s, g_re, g_im):
        zero = jnp.zeros((N, HALF), F32)
        lefts, rights = [], []
        for part, g in ((0, g_re), (1, g_im)):
            moved = pltpu.roll(g, lax.rem(off_x + N - MARGIN, N), 1)
            low, high = moved[:, :HALF], moved[:, HALF:]
            rights.append(jnp.where(over_right, low, zero))
            lefts.append(jnp.where(over_left, high, zero))
            kept = [jnp.where(over_right, zero, low), jnp.where(over_left, zero, high)]
            gmid[s, part] = down(jnp.concatenate(kept, axis=1), off_y)
        gpick[s] = right_margin(*lefts) + left_margin(*rights)

    def fold_side(s):
        return remote(gpick.at[s], gside.at[s], fold_send.at[s, 5], fold_recv.at[s, 5], pair_peer)

    def fold_hops(s):
        moves = (
            (ghop.at[s, inner, :], rhop.at[s], (0, -hop_to)),
            (ghop.at[s, top, :], rcor.at[s, 0], (-1, -hop_to)),
            (ghop.at[s, bottom, :], rcor.at[s, 1], (1, -hop_to)),
        )
        return [remote(src, dst, fold_send.at[s, i], fold_recv.at[s, i], neighbour(*step))
                for i, (src, dst, step) in enumerate(moves)]

    def fold_rows(s):
        moves = (
            (gmid.at[s, :, top, :], rrow.at[s, 0], (-1, 0)),
            (gmid.at[s, :, bottom, :], rrow.at[s, 1], (1, 0)),
        )
        return [remote(src, dst, fold_send.at[s, 3 + i], fold_recv.at[s, 3 + i], neighbour(*step))
                for i, (src, dst, step) in enumerate(moves)]

    fsides, fhops, frows = ([f(s) for s in (0, 1)] for f in (fold_side, fold_hops, fold_rows))

    def add_packed(ref, s, place, packed, lefthand):
        low = lower[:packed.shape[0]]
        turned = pltpu.roll(packed, 64, 1)
        if lefthand:
            ref[s, 0, place, :HALF] += jnp.where(low, packed, 0.0)
            ref[s, 1, place, :HALF] += jnp.where(low, turned, 0.0)
        else:
            ref[s, 0, place, HALF:] += jnp.where(low, 0.0, turned)
            ref[s, 1, place, HALF:] += jnp.where(low, 0.0, packed)

    def pass_on(s):
        fsides[s].wait_recv()
        got = down(gside[s], peer_offs[0, 0, 0, 0])
        own = peer_takes_own((EXT, HALF))
        ghop[s] = jnp.where(own, 0.0, got)
        here = jnp.where(own, got, 0.0)

        @pl.when(z_lo == 0)
        def _():
            add_packed(gmid, s, pl.ds(0, EXT), here, False)

        @pl.when(z_lo == 1)
        def _():
            add_packed(gmid, s, pl.ds(0, EXT), here, True)

    first, last = pl.ds(0, MARGIN), pl.ds(N - MARGIN, MARGIN)

    def collect(s):
        for copy in fhops[s] + frows[s]:
            copy.wait_recv()
        for part in (0, 1):
            owned[s, part] = gmid[s, part, inner, :]

        @pl.when(row < rows - 1)
        def _():
            owned[s, :, last, :] += rrow[s, 0]

        @pl.when(row > 0)
        def _():
            owned[s, :, first, :] += rrow[s, 1]

        for lo, valid in ((0, col > 0), (1, col < cols - 1)):
            @pl.when(jnp.logical_and(z_lo == lo, valid))
            def _():
                add_packed(owned, s, pl.ds(0, N), rhop[s], lo == 0)

                @pl.when(row < rows - 1)
                def _():
                    add_packed(owned, s, last, rcor[s, 0], lo == 0)

                @pl.when(row > 0)
                def _():
                    add_packed(owned, s, first, rcor[s, 1], lo == 0)

    exchange.wait_recv()
    for copy in halo_row[0] + hops[0]:
        copy.wait_recv()
    clear_edges(0)
    choose(0)
    sides[0].start()
    for copy in halo_row[1] + hops[1]:
        copy.wait_recv()
    clear_edges(1)
    choose(1)
    sides[1].start()
    sides[0].wait_recv()
    window(0, win1)
    entry = product(probe[0], probe[1], win1[0], win1[1])
    spectrum = forward(*entry, tabs)
    moved = product(kern[0], kern[1], *spectrum)
    arrive[0], arrive[1] = inverse(*moved, tabs)

    sides[1].wait_recv()
    window(1, win2)
    far_re, far_im = forward(*product(arrive[0], arrive[1], win2[0], win2[1]), tabs)
    factor = 2.0 - 2.0 * amp[...] * lax.rsqrt(far_re * far_re + far_im * far_im + EPS_AMP)
    back_re, back_im = inverse(factor * far_re, factor * far_im, tabs)
    spread(1, *conj_product(arrive[0], arrive[1], back_re, back_im))
    fsides[1].start()
    spec = forward(*conj_product(win2[0], win2[1], back_re, back_im), tabs)
    ent_re, ent_im = inverse(*conj_product(kern[0], kern[1], *spec), tabs)
    gprobe[0], gprobe[1] = conj_product(win1[0], win1[1], ent_re, ent_im)

    both_cores = remote(gprobe.at[1 - core], recv_a, ar_send.at[0, 0], ar_recv.at[0, 0], partner)
    both_cores.start()
    spread(0, *conj_product(probe[0], probe[1], ent_re, ent_im))
    fsides[0].start()
    both_cores.wait_recv()
    half[...] = gprobe[core] + recv_a[...]

    def scatter(k):
        return remote(half.at[pl.ds(pl.multiple_of(plane_at(k) * share, share), share), :], recv_b.at[k],
                      ar_send.at[1, k], ar_recv.at[1, k], plane_peer(k))

    for k in plane_steps:
        scatter(k).start()
    mine = pl.ds(pl.multiple_of(plane * share, share), share)
    recv_b[0] = half[mine, :]
    pass_on(1)
    for copy in frows[1] + fhops[1][1:]:
        copy.start()
    pass_on(0)
    for k in plane_steps:
        scatter(k).wait_recv()
    total = recv_b[0]
    for k in range(1, planes):
        total = total + recv_b[k]
    sum_b[...] = total

    def across(k):
        return remote(sum_b, recv_c.at[z], ar_send.at[2, k], ar_recv.at[2, k], z_peer(k))

    for k in z_steps:
        across(k).start()
    fhops[1][0].start()
    fhops[0][0].start()
    for k in z_steps:
        across(k).wait_send()
    for copy in frows[0] + fhops[0][1:]:
        copy.start()
    recv_c[z] = total
    for k in z_steps:
        across(k).wait_recv()
    total = recv_c[0]
    for d in range(1, zs):
        total = total + recv_c[d]
    final[mine, :] = total

    def gather(k):
        return remote(final.at[mine, :], final.at[mine, :], ar_send.at[3, k], ar_recv.at[3, k], plane_peer(k))

    def hand_over(k):
        place = pl.ds(pl.multiple_of(plane_at(k, -1) * share, share), share)
        return remote(final.at[place, :], probe_out.at[core, place, :], ar_send.at[4, k], ar_recv.at[4, k], partner)

    for k in plane_steps:
        gather(k).start()
    hand_over(0).start()
    for s in (0, 1):
        for copy in [*hops[s], sides[s], fsides[s]]:
            copy.wait_send()
    for copy in halo_row[1] + fhops[1] + frows[1]:
        copy.wait_send()
    exchange.wait_send()
    both_cores.wait_send()
    for k in plane_steps:
        scatter(k).wait_send()
    for k in reversed(plane_steps):
        gather(k).wait_recv()
        hand_over(k).start()
    store2 = pltpu.make_async_copy(final, probe_out.at[core], out_sem.at[2])
    store2.start()
    collect(1)
    store1 = pltpu.make_async_copy(owned.at[1], obj_out.at[1], out_sem.at[1])
    store1.start()
    collect(0)
    store0 = pltpu.make_async_copy(owned.at[0], obj_out.at[0], out_sem.at[0])
    store0.start()
    for k in range(planes):
        hand_over(k).wait_recv()

    for copy in frows[0] + fhops[0]:
        copy.wait_send()
    for k in plane_steps:
        gather(k).wait_send()
    for k in range(planes):
        hand_over(k).wait_send()
    store0.wait()
    store1.wait()
    store2.wait()


def place_outputs(obj, probe, obj_out, probe_out, held, load_sem, store_sem):
    places = [(obj, obj_out, (i, j)) for i in (0, 1) for j in (0, 1)] + [(probe, probe_out, (i,)) for i in (0, 1)]
    loads = [pltpu.make_async_copy(src.at[at], held.at[k], load_sem.at[k]) for k, (src, _, at) in enumerate(places)]
    stores = [pltpu.make_async_copy(held.at[k], dst.at[at], store_sem.at[k]) for k, (_, dst, at) in enumerate(places)]
    for load in loads:
        load.start()
    for load, store in zip(loads, stores):
        load.wait()
        store.start()
    for store in stores:
        store.wait()


def body(rows, cols, object_field, probe, phase, amplitudes, offsets):
    planes, zs = cols // 2, rows
    share = N // planes
    vmem = lambda *shape: pltpu.VMEM(shape, F32)
    dma = pltpu.SemaphoreType.DMA
    hbm = pl.BlockSpec(memory_space=pl.ANY)
    grads = pl.pallas_call(
        functools.partial(kernel, rows, cols),
        out_shape=(
            jax.ShapeDtypeStruct((2, 2, N, N), F32),
            jax.ShapeDtypeStruct((2, N, N), F32),
        ),
        in_specs=[hbm, hbm, hbm, hbm, pl.BlockSpec(memory_space=pltpu.SMEM), hbm, hbm],
        out_specs=(hbm, hbm),
        scratch_shapes=[
            vmem(2, 2, EXT, N),
            vmem(2, N, HALF),
            vmem(2, EXT, HALF),
            vmem(2, N, HALF),
            vmem(2, N, HALF),
            vmem(2, N, N),
            vmem(N, N),
            vmem(N, N),
            pltpu.VMEM((4, 2 * N, N), BF16),
            pltpu.VMEM((2, N, N), BF16),
            pltpu.SMEM((1, 1, 1, 2), jnp.int32),
            vmem(2, N, N),
            vmem(2, N, N),
            vmem(2, N, N),
            vmem(2, N, N),
            vmem(2, 2, EXT, N),
            vmem(2, N, HALF),
            vmem(2, N, HALF),
            vmem(2, EXT, HALF),
            vmem(2, 2, 2, MARGIN, N),
            vmem(2, N, HALF),
            vmem(2, 2, MARGIN, HALF),
            vmem(2, N, N),
            vmem(N, N),
            vmem(N, N),
            vmem(planes, share, N),
            vmem(share, N),
            vmem(zs, share, N),
            vmem(N, N),
            vmem(2, 2, N, N),
            dma((7,)),
            dma((2,)),
            dma((2, 6)),
            dma((2, 6)),
            dma((2, 6)),
            dma((2, 6)),
            dma((5, 16)),
            dma((5, 16)),
            dma((3,)),
        ],
        compiler_params=pltpu.CompilerParams(
            collective_id=0, has_side_effects=True, vmem_limit_bytes=63 * 1024 * 1024
        ),
    )(object_field, probe, phase, amplitudes, offsets, jnp.asarray(dft_constants()), jnp.asarray(order_constant()))
    return pl.pallas_call(
        place_outputs,
        out_shape=(
            jax.ShapeDtypeStruct((2, 2, N, N), F32),
            jax.ShapeDtypeStruct((2, N, N), F32),
        ),
        in_specs=[hbm, hbm],
        out_specs=(hbm, hbm),
        scratch_shapes=[vmem(6, N, N), dma((6,)), dma((6,))],
        compiler_params=pltpu.CompilerParams(vmem_limit_bytes=63 * 1024 * 1024),
    )(*grads)


def solution(mesh):
    placed = (
        P(None, None, "row", "col"),
        P(),
        P(),
        P("row", "col", None, None, None),
        P("row", "col", None, None),
    )
    return jax.shard_map(
        functools.partial(body, mesh.shape["row"], mesh.shape["col"]),
        mesh=mesh,
        in_specs=placed,
        out_specs=(P(None, None, "row", "col"), P()),
        check_vma=False,
    )
```

```python
import functools
import math

import jax
import jax.numpy as jnp
import ml_dtypes
import numpy as np
from jax import lax
from jax.experimental import pallas as pl
from jax.experimental.pallas import tpu as pltpu
from jax.sharding import PartitionSpec as P

EPS_AMP = 0.5
MESH = pl.DeviceIdType.MESH
N = 256
HALF = N // 2
MARGIN = 64
EXT = N + 2 * MARGIN
F32 = jnp.float32
BF16 = jnp.bfloat16


def dft_constants():
    j = np.arange(HALF)[:, None]
    k = np.arange(HALF)[None, :]
    mats = []
    for odd in (0, 1):
        angle = -2.0 * np.pi * (((2 * j + odd) * k) % N) / N
        re, im = np.cos(angle) / 16.0, np.sin(angle) / 16.0
        mats.append(np.block([[re, -im], [im, re]]))
    mats += [mats[0].T, mats[1].T]
    out = []
    for m in mats:
        hi = m.astype(ml_dtypes.bfloat16)
        lo = (m - hi.astype(np.float64)).astype(ml_dtypes.bfloat16)
        out.append(np.concatenate([hi, lo], axis=0))
    return np.stack(out)


def order_constant():
    q = np.zeros((N, N), np.float32)
    q[np.arange(HALF), 2 * np.arange(HALF)] = 1.0
    q[HALF + np.arange(HALF), 2 * np.arange(HALF) + 1] = 1.0
    return np.stack([q, q.T]).astype(ml_dtypes.bfloat16)


def dot(a, b):
    return jnp.dot(a, b, preferred_element_type=F32)


def two_terms(x):
    hi = x.astype(BF16)
    return hi, (x - hi.astype(F32)).astype(BF16)


def left_apply(table, x):
    hi, lo = two_terms(x)
    both = dot(table[...], hi)
    return both[:N] + both[N:] + dot(table[:N], lo)


def right_apply(x, table):
    hi, lo = two_terms(x)
    return dot(hi, table[:N]) + dot(lo, table[:N]) + dot(hi, table[N:])


def left_forward(x_re, x_im, tabs):
    low = jnp.concatenate([x_re[:HALF], x_im[:HALF]], axis=0)
    high = jnp.concatenate([x_re[HALF:], x_im[HALF:]], axis=0)
    even = left_apply(tabs.at[0], low + high)
    odd = left_apply(tabs.at[1], low - high)
    return (
        jnp.concatenate([even[:HALF], odd[:HALF]], axis=0),
        jnp.concatenate([even[HALF:], odd[HALF:]], axis=0),
    )


def right_forward(x_re, x_im, tabs):
    low = jnp.concatenate([x_re[:, :HALF], x_im[:, :HALF]], axis=1)
    high = jnp.concatenate([x_re[:, HALF:], x_im[:, HALF:]], axis=1)
    even = right_apply(low + high, tabs.at[2])
    odd = right_apply(low - high, tabs.at[3])
    return (
        jnp.concatenate([even[:, :HALF], odd[:, :HALF]], axis=1),
        jnp.concatenate([even[:, HALF:], odd[:, HALF:]], axis=1),
    )


def left_inverse(x_re, x_im, tabs):
    a = left_apply(tabs.at[2], jnp.concatenate([x_re[:HALF], x_im[:HALF]], axis=0))
    b = left_apply(tabs.at[3], jnp.concatenate([x_re[HALF:], x_im[HALF:]], axis=0))
    low, high = a + b, a - b
    return (
        jnp.concatenate([low[:HALF], high[:HALF]], axis=0),
        jnp.concatenate([low[HALF:], high[HALF:]], axis=0),
    )


def right_inverse(x_re, x_im, tabs):
    a = right_apply(jnp.concatenate([x_re[:, :HALF], x_im[:, :HALF]], axis=1), tabs.at[0])
    b = right_apply(jnp.concatenate([x_re[:, HALF:], x_im[:, HALF:]], axis=1), tabs.at[1])
    low, high = a + b, a - b
    return (
        jnp.concatenate([low[:, :HALF], high[:, :HALF]], axis=1),
        jnp.concatenate([low[:, HALF:], high[:, HALF:]], axis=1),
    )


def forward(x_re, x_im, tabs):
    return right_forward(*left_forward(x_re, x_im, tabs), tabs)


def inverse(x_re, x_im, tabs):
    return right_inverse(*left_inverse(x_re, x_im, tabs), tabs)


class Move:
    def __init__(self, copy, sends, arrives):
        self.copy, self.sends, self.arrives = copy, sends, arrives

    def start(self):
        pl.when(self.sends)(self.copy.start)

    def wait_send(self):
        pl.when(self.sends)(self.copy.wait_send)

    def wait_recv(self):
        pl.when(self.arrives)(self.copy.wait_recv)


def product(a_re, a_im, b_re, b_im):
    return a_re * b_re - a_im * b_im, a_re * b_im + a_im * b_re


def conj_product(a_re, a_im, b_re, b_im):
    return a_re * b_re + a_im * b_im, a_re * b_im - a_im * b_re


def reorder(x, order):
    hi = x.astype(BF16)
    rest = x - hi.astype(F32)
    mid = rest.astype(BF16)
    low = (rest - mid.astype(F32)).astype(BF16)
    parts = []
    for term in (hi, mid, low):
        rows = dot(order[0], term).astype(BF16)
        parts.append(dot(rows, order[1]))
    return parts[0] + parts[1] + parts[2]


def cos_sin(x):
    h = 0.5 * x
    t = h * h
    s = h * (1.0 + t * (-1.0 / 6 + t * (1.0 / 120 + t * (-1.0 / 5040 + t * (
        1.0 / 362880 + t * (-1.0 / 39916800 + t * (1.0 / 6227020800)))))))
    c = 1.0 + t * (-0.5 + t * (1.0 / 24 + t * (-1.0 / 720 + t * (1.0 / 40320 + t * (
        -1.0 / 3628800 + t * (1.0 / 479001600 + t * (-1.0 / 87178291200)))))))
    return 1.0 - 2.0 * s * s, 2.0 * s * c


def kernel(
    rows, cols,
    obj, probe_in, phase_in, amp_in, offs, tabs_in, order_in,
    obj_out, probe_out,
    mid, pack, hop, pick, side, probe, phase, amp, tabs, order, peer_offs, win1, win2, arrive, kern,
    gmid, gpick, gside, ghop, rrow, rhop, rcor, gprobe, recv_a, half, recv_b, sum_b, recv_c, final, owned,
    in_sem, offs_sem, halo_send, halo_recv, fold_send, fold_recv, ar_send, ar_recv, out_sem,
):
    row, col = lax.axis_index("row"), lax.axis_index("col")
    core, z_hi = row % 2, row // 2
    plane, z_lo = col // 2, col % 2
    planes, zs = cols // 2, rows
    z = z_hi * 2 + z_lo
    share = N // planes

    def neighbour(dr, dc):
        return ((row + dr + rows) % rows, (col + dc + cols) % cols)

    hop_to = 4 * z_lo - 2
    pair_peer = (row, col + 1 - 2 * z_lo)
    partner = (z_hi * 2 + 1 - core, col)

    side_len = math.isqrt(planes)
    far = lambda step, length: min(step, length - step)
    plane_steps = sorted(
        range(1, planes), key=lambda k: -far(k // side_len, side_len) - far(k % side_len, side_len))
    z_steps = sorted(range(1, zs), key=lambda k: -far(k, zs))

    def plane_at(k, sign=1):
        x, y = plane // side_len, plane % side_len
        return (x + side_len + sign * (k // side_len)) % side_len * side_len + (y + side_len + sign * (k % side_len)) % side_len

    def plane_peer(k):
        return (row, plane_at(k) * 2 + z_lo)

    def z_peer(k):
        other = (z + k) % zs
        return ((other // 2) * 2 + core, plane * 2 + other % 2)

    barrier = pltpu.get_barrier_semaphore()
    for step in ((-1, 0), (1, 0), (-1, -2), (-1, 2), (1, -2), (1, 2)):
        pl.semaphore_signal(barrier, inc=1, device_id=neighbour(*step), device_id_type=MESH)

    for k in plane_steps:
        pl.semaphore_signal(barrier, inc=1, device_id=plane_peer(k), device_id_type=MESH)
    for k in z_steps:
        pl.semaphore_signal(barrier, inc=1, device_id=z_peer(k), device_id_type=MESH)

    loads = [
        pltpu.make_async_copy(obj.at[0], mid.at[0, :, pl.ds(MARGIN, N), :], in_sem.at[0]),
        pltpu.make_async_copy(obj.at[1], mid.at[1, :, pl.ds(MARGIN, N), :], in_sem.at[1]),
        pltpu.make_async_copy(probe_in, probe, in_sem.at[2]),
        pltpu.make_async_copy(phase_in, phase, in_sem.at[3]),
        pltpu.make_async_copy(order_in, order, in_sem.at[4]),
        pltpu.make_async_copy(amp_in.at[0, 0, 0], amp, in_sem.at[5]),
        pltpu.make_async_copy(tabs_in, tabs, in_sem.at[6]),
    ]
    for load in loads:
        load.start()

    lane = lax.broadcasted_iota(jnp.int32, (N, HALF), 1)
    lower = lax.broadcasted_iota(jnp.int32, (EXT, HALF), 1) < 64

    def left_margin(re, im):
        return jnp.where(lower[:re.shape[0]], re, pltpu.roll(im, 64, 1))

    def right_margin(re, im):
        return jnp.where(lower[:re.shape[0]], pltpu.roll(re, 64, 1), im)

    def pack_outer(s):
        inner = pl.ds(MARGIN, N)

        @pl.when(z_lo == 0)
        def _():
            pack[s] = left_margin(mid[s, 0, inner, :HALF], mid[s, 1, inner, :HALF])

        @pl.when(z_lo == 1)
        def _():
            pack[s] = right_margin(mid[s, 0, inner, HALF:], mid[s, 1, inner, HALF:])

    def remote(src, dst, send, recv, device):
        return pltpu.make_async_remote_copy(
            src_ref=src, dst_ref=dst, send_sem=send, recv_sem=recv, device_id=device, device_id_type=MESH)

    def within(dr, dc):
        here, there = row + dr, col + dc
        return jnp.logical_and(
            jnp.logical_and(here >= 0, here < rows), jnp.logical_and(there >= 0, there < cols))

    def to_neighbour(src, dst, send, recv, dr, dc):
        return Move(remote(src, dst, send, recv, neighbour(dr, dc)), within(dr, dc), within(-dr, -dc))

    top, inner, bottom = pl.ds(0, MARGIN), pl.ds(MARGIN, N), pl.ds(MARGIN + N, MARGIN)

    def halo_hops(s):
        moves = (
            (pack.at[s], hop.at[s, inner, :], (0, hop_to)),
            (pack.at[s, pl.ds(0, MARGIN), :], hop.at[s, bottom, :], (-1, hop_to)),
            (pack.at[s, pl.ds(N - MARGIN, MARGIN), :], hop.at[s, top, :], (1, hop_to)),
        )
        return [to_neighbour(src, dst, halo_send.at[s, i], halo_recv.at[s, i], *step)
                for i, (src, dst, step) in enumerate(moves)]

    def halo_rows(s):
        moves = (
            (obj.at[s, :, pl.ds(0, MARGIN), :], mid.at[s, :, bottom, :], (-1, 0)),
            (obj.at[s, :, pl.ds(N - MARGIN, MARGIN), :], mid.at[s, :, top, :], (1, 0)),
        )
        return [to_neighbour(src, dst, halo_send.at[s, 3 + i], halo_recv.at[s, 3 + i], *step)
                for i, (src, dst, step) in enumerate(moves)]

    def halo_side(s):
        return remote(pick.at[s], side.at[s], halo_send.at[s, 5], halo_recv.at[s, 5], pair_peer)

    hops, halo_row, sides = ([f(s) for s in (0, 1)] for f in (halo_hops, halo_rows, halo_side))
    exchange = remote(offs, peer_offs, offs_sem.at[0], offs_sem.at[1], pair_peer)
    pl.semaphore_wait(barrier, 6 + planes - 1 + zs - 1)
    for copy in halo_row[0]:
        copy.start()
    exchange.start()
    loads[0].wait()
    pack_outer(0)
    for copy in hops[0]:
        copy.start()
    loads[1].wait()
    pack_outer(1)
    hops[1][0].start()
    loads[3].wait()
    loads[4].wait()
    kern[0], kern[1] = cos_sin(reorder(phase[...], order))
    loads[5].wait()
    amp[...] = reorder(amp[...], order)
    loads[2].wait()
    loads[6].wait()

    @pl.when(jnp.logical_not(within(0, -hop_to)))
    def _():
        hop[...] = jnp.zeros_like(hop)

    for copy in halo_row[0]:
        copy.wait_send()
    for copy in halo_row[1] + hops[1][1:]:
        copy.start()
    off_y, off_x = offs[0, 0, 0, 0], offs[0, 0, 0, 1]
    shift = off_x - MARGIN

    outside = jnp.logical_or(
        jnp.logical_and(col == 0, off_x < MARGIN), jnp.logical_and(col == cols - 1, off_x > MARGIN))
    inside = 1.0 - outside.astype(F32)

    def clear_edges(s):
        @pl.when(row == 0)
        def _():
            mid[s, :, top, :] = jnp.zeros((2, MARGIN, N), F32)
            hop[s, top, :] = jnp.zeros((MARGIN, HALF), F32)

        @pl.when(row == rows - 1)
        def _():
            mid[s, :, bottom, :] = jnp.zeros((2, MARGIN, N), F32)
            hop[s, bottom, :] = jnp.zeros((MARGIN, HALF), F32)

    def up(x, amount):
        return pltpu.roll(x, lax.rem(EXT - amount, EXT), 0)[:N]

    def down(x, amount):
        below = jnp.zeros((EXT - N, x.shape[1]), F32)
        return pltpu.roll(jnp.concatenate([x, below], axis=0), amount, 0)

    def peer_takes_own(shape):
        reach = (peer_offs[0, 0, 0, 1] - MARGIN) * (1 - 2 * z_lo)
        return lax.broadcasted_iota(jnp.int32, shape, 1) * 0 + reach < 0

    def choose(s):
        own = peer_takes_own((EXT, HALF))

        @pl.when(z_lo == 0)
        def _():
            mine = right_margin(mid[s, 0, :, HALF:], mid[s, 1, :, HALF:])
            pick[s] = up(jnp.where(own, mine, hop[s]), peer_offs[0, 0, 0, 0])

        @pl.when(z_lo == 1)
        def _():
            mine = left_margin(mid[s, 0, :, :HALF], mid[s, 1, :, :HALF])
            pick[s] = up(jnp.where(own, mine, hop[s]), peer_offs[0, 0, 0, 0])

    over_right, over_left = lane < shift, lane >= HALF + shift

    def window(s, ref):
        beside = side[s] * inside
        turned = pltpu.roll(beside, 64, 1)
        for part in (0, 1):
            both = up(mid[s, part], off_y)
            low = jnp.where(over_right, beside if part == 0 else turned, both[:, :HALF])
            high = jnp.where(over_left, turned if part == 0 else beside, both[:, HALF:])
            ref[part] = pltpu.roll(jnp.concatenate([low, high], axis=1), lax.rem(N + MARGIN - off_x, N), 1)

    def spread(s, g_re, g_im):
        zero = jnp.zeros((N, HALF), F32)
        lefts, rights = [], []
        for part, g in ((0, g_re), (1, g_im)):
            moved = pltpu.roll(g, lax.rem(off_x + N - MARGIN, N), 1)
            low, high = moved[:, :HALF], moved[:, HALF:]
            rights.append(jnp.where(over_right, low, zero))
            lefts.append(jnp.where(over_left, high, zero))
            kept = [jnp.where(over_right, zero, low), jnp.where(over_left, zero, high)]
            gmid[s, part] = down(jnp.concatenate(kept, axis=1), off_y)
        gpick[s] = right_margin(*lefts) + left_margin(*rights)

    def fold_side(s):
        return remote(gpick.at[s], gside.at[s], fold_send.at[s, 5], fold_recv.at[s, 5], pair_peer)

    def fold_hops(s):
        moves = (
            (ghop.at[s, inner, :], rhop.at[s], (0, -hop_to)),
            (ghop.at[s, top, :], rcor.at[s, 0], (-1, -hop_to)),
            (ghop.at[s, bottom, :], rcor.at[s, 1], (1, -hop_to)),
        )
        return [to_neighbour(src, dst, fold_send.at[s, i], fold_recv.at[s, i], *step)
                for i, (src, dst, step) in enumerate(moves)]

    def fold_rows(s):
        moves = (
            (gmid.at[s, :, top, :], rrow.at[s, 0], (-1, 0)),
            (gmid.at[s, :, bottom, :], rrow.at[s, 1], (1, 0)),
        )
        return [to_neighbour(src, dst, fold_send.at[s, 3 + i], fold_recv.at[s, 3 + i], *step)
                for i, (src, dst, step) in enumerate(moves)]

    fsides, fhops, frows = ([f(s) for s in (0, 1)] for f in (fold_side, fold_hops, fold_rows))

    def add_packed(ref, s, place, packed, lefthand):
        low = lower[:packed.shape[0]]
        turned = pltpu.roll(packed, 64, 1)
        if lefthand:
            ref[s, 0, place, :HALF] += jnp.where(low, packed, 0.0)
            ref[s, 1, place, :HALF] += jnp.where(low, turned, 0.0)
        else:
            ref[s, 0, place, HALF:] += jnp.where(low, 0.0, turned)
            ref[s, 1, place, HALF:] += jnp.where(low, 0.0, packed)

    def pass_on(s):
        fsides[s].wait_recv()
        got = down(gside[s], peer_offs[0, 0, 0, 0])
        own = peer_takes_own((EXT, HALF))
        ghop[s] = jnp.where(own, 0.0, got)
        here = jnp.where(own, got, 0.0)

        @pl.when(z_lo == 0)
        def _():
            add_packed(gmid, s, pl.ds(0, EXT), here, False)

        @pl.when(z_lo == 1)
        def _():
            add_packed(gmid, s, pl.ds(0, EXT), here, True)

    first, last = pl.ds(0, MARGIN), pl.ds(N - MARGIN, MARGIN)

    def collect(s):
        for copy in fhops[s] + frows[s]:
            copy.wait_recv()
        for part in (0, 1):
            owned[s, part] = gmid[s, part, inner, :]

        @pl.when(row < rows - 1)
        def _():
            owned[s, :, last, :] += rrow[s, 0]

        @pl.when(row > 0)
        def _():
            owned[s, :, first, :] += rrow[s, 1]

        for lo, valid in ((0, col > 0), (1, col < cols - 1)):
            @pl.when(jnp.logical_and(z_lo == lo, valid))
            def _():
                add_packed(owned, s, pl.ds(0, N), rhop[s], lo == 0)

                @pl.when(row < rows - 1)
                def _():
                    add_packed(owned, s, last, rcor[s, 0], lo == 0)

                @pl.when(row > 0)
                def _():
                    add_packed(owned, s, first, rcor[s, 1], lo == 0)

    exchange.wait_recv()
    for copy in halo_row[0] + hops[0]:
        copy.wait_recv()
    clear_edges(0)
    choose(0)
    sides[0].start()
    for copy in halo_row[1] + hops[1]:
        copy.wait_recv()
    clear_edges(1)
    choose(1)
    sides[1].start()
    sides[0].wait_recv()
    window(0, win1)
    entry = product(probe[0], probe[1], win1[0], win1[1])
    spectrum = forward(*entry, tabs)
    moved = product(kern[0], kern[1], *spectrum)
    arrive[0], arrive[1] = inverse(*moved, tabs)

    sides[1].wait_recv()
    window(1, win2)
    far_re, far_im = forward(*product(arrive[0], arrive[1], win2[0], win2[1]), tabs)
    factor = 2.0 - 2.0 * amp[...] * lax.rsqrt(far_re * far_re + far_im * far_im + EPS_AMP)
    back_re, back_im = inverse(factor * far_re, factor * far_im, tabs)
    spread(1, *conj_product(arrive[0], arrive[1], back_re, back_im))
    fsides[1].start()
    spec = forward(*conj_product(win2[0], win2[1], back_re, back_im), tabs)
    ent_re, ent_im = inverse(*conj_product(kern[0], kern[1], *spec), tabs)
    gprobe[0], gprobe[1] = conj_product(win1[0], win1[1], ent_re, ent_im)

    both_cores = remote(gprobe.at[1 - core], recv_a, ar_send.at[0, 0], ar_recv.at[0, 0], partner)
    both_cores.start()
    spread(0, *conj_product(probe[0], probe[1], ent_re, ent_im))
    fsides[0].start()
    both_cores.wait_recv()
    half[...] = gprobe[core] + recv_a[...]

    def scatter(k):
        return remote(half.at[pl.ds(pl.multiple_of(plane_at(k) * share, share), share), :], recv_b.at[k],
                      ar_send.at[1, k], ar_recv.at[1, k], plane_peer(k))

    for k in plane_steps:
        scatter(k).start()
    mine = pl.ds(pl.multiple_of(plane * share, share), share)
    recv_b[0] = half[mine, :]
    pass_on(1)
    for copy in frows[1] + fhops[1]:
        copy.start()
    for k in plane_steps:
        scatter(k).wait_recv()
    total = recv_b[0]
    for k in range(1, planes):
        total = total + recv_b[k]
    sum_b[...] = total

    def across(k):
        return remote(sum_b, recv_c.at[z], ar_send.at[2, k], ar_recv.at[2, k], z_peer(k))

    for k in z_steps:
        across(k).start()
    pass_on(0)
    fhops[0][0].start()
    for k in z_steps:
        across(k).wait_send()
    for copy in frows[0] + fhops[0][1:]:
        copy.start()
    recv_c[z] = total
    for k in z_steps:
        across(k).wait_recv()
    total = recv_c[0]
    for d in range(1, zs):
        total = total + recv_c[d]
    final[mine, :] = total

    def gather(k):
        return remote(final.at[mine, :], final.at[mine, :], ar_send.at[3, k], ar_recv.at[3, k], plane_peer(k))

    def hand_over(k):
        place = pl.ds(pl.multiple_of(plane_at(k, -1) * share, share), share)
        return remote(final.at[place, :], probe_out.at[core, place, :], ar_send.at[4, k], ar_recv.at[4, k], partner)

    for k in plane_steps:
        gather(k).start()
    hand_over(0).start()
    for s in (0, 1):
        for copy in [*hops[s], sides[s], fsides[s]]:
            copy.wait_send()
    for copy in halo_row[1] + fhops[1] + frows[1]:
        copy.wait_send()
    exchange.wait_send()
    both_cores.wait_send()
    for k in plane_steps:
        scatter(k).wait_send()
    collect(1)
    store1 = pltpu.make_async_copy(owned.at[1], obj_out.at[1], out_sem.at[1])
    store1.start()
    early = plane_steps[::-1][:10]
    for k in early:
        gather(k).wait_recv()
        hand_over(k).start()
    collect(0)
    store0 = pltpu.make_async_copy(owned.at[0], obj_out.at[0], out_sem.at[0])
    store0.start()
    for k in plane_steps[::-1][10:]:
        gather(k).wait_recv()
        hand_over(k).start()
    store2 = pltpu.make_async_copy(final, probe_out.at[core], out_sem.at[2])
    store2.start()
    for k in range(planes):
        hand_over(k).wait_recv()

    for copy in frows[0] + fhops[0]:
        copy.wait_send()
    for k in plane_steps:
        gather(k).wait_send()
    for k in range(planes):
        hand_over(k).wait_send()
    store0.wait()
    store1.wait()
    store2.wait()


def place_outputs(obj, probe, obj_out, probe_out, held, load_sem, store_sem):
    count = held.shape[0] // 6
    pieces = [pl.ds(i * (N // count), N // count) for i in range(count)]
    places = [(obj, obj_out, (i, j, piece)) for i in (0, 1) for j in (0, 1) for piece in pieces]
    places += [(probe, probe_out, (i, piece)) for i in (0, 1) for piece in pieces]
    loads = [pltpu.make_async_copy(src.at[at], held.at[k], load_sem.at[k]) for k, (src, _, at) in enumerate(places)]
    stores = [pltpu.make_async_copy(held.at[k], dst.at[at], store_sem.at[k]) for k, (_, dst, at) in enumerate(places)]
    for load in loads:
        load.start()
    for load, store in zip(loads, stores):
        load.wait()
        store.start()
    for store in stores:
        store.wait()


def body(rows, cols, object_field, probe, phase, amplitudes, offsets):
    planes, zs = cols // 2, rows
    share = N // planes
    vmem = lambda *shape: pltpu.VMEM(shape, F32)
    dma = pltpu.SemaphoreType.DMA
    hbm = pl.BlockSpec(memory_space=pl.ANY)
    grads = pl.pallas_call(
        functools.partial(kernel, rows, cols),
        out_shape=(
            jax.ShapeDtypeStruct((2, 2, N, N), F32),
            jax.ShapeDtypeStruct((2, N, N), F32),
        ),
        in_specs=[hbm, hbm, hbm, hbm, pl.BlockSpec(memory_space=pltpu.SMEM), hbm, hbm],
        out_specs=(hbm, hbm),
        scratch_shapes=[
            vmem(2, 2, EXT, N),
            vmem(2, N, HALF),
            vmem(2, EXT, HALF),
            vmem(2, N, HALF),
            vmem(2, N, HALF),
            vmem(2, N, N),
            vmem(N, N),
            vmem(N, N),
            pltpu.VMEM((4, 2 * N, N), BF16),
            pltpu.VMEM((2, N, N), BF16),
            pltpu.SMEM((1, 1, 1, 2), jnp.int32),
            vmem(2, N, N),
            vmem(2, N, N),
            vmem(2, N, N),
            vmem(2, N, N),
            vmem(2, 2, EXT, N),
            vmem(2, N, HALF),
            vmem(2, N, HALF),
            vmem(2, EXT, HALF),
            vmem(2, 2, 2, MARGIN, N),
            vmem(2, N, HALF),
            vmem(2, 2, MARGIN, HALF),
            vmem(2, N, N),
            vmem(N, N),
            vmem(N, N),
            vmem(planes, share, N),
            vmem(share, N),
            vmem(zs, share, N),
            vmem(N, N),
            vmem(2, 2, N, N),
            dma((7,)),
            dma((2,)),
            dma((2, 6)),
            dma((2, 6)),
            dma((2, 6)),
            dma((2, 6)),
            dma((5, 16)),
            dma((5, 16)),
            dma((3,)),
        ],
        compiler_params=pltpu.CompilerParams(
            collective_id=0, has_side_effects=True, vmem_limit_bytes=63 * 1024 * 1024
        ),
    )(object_field, probe, phase, amplitudes, offsets, jnp.asarray(dft_constants()), jnp.asarray(order_constant()))
    return pl.pallas_call(
        place_outputs,
        out_shape=(
            jax.ShapeDtypeStruct((2, 2, N, N), F32),
            jax.ShapeDtypeStruct((2, N, N), F32),
        ),
        in_specs=[hbm, hbm],
        out_specs=(hbm, hbm),
        scratch_shapes=[vmem(6 * 1, N // 1, N), dma((6 * 1,)), dma((6 * 1,))],
        compiler_params=pltpu.CompilerParams(vmem_limit_bytes=63 * 1024 * 1024),
    )(*grads)


def solution(mesh):
    placed = (
        P(None, None, "row", "col"),
        P(),
        P(),
        P("row", "col", None, None, None),
        P("row", "col", None, None),
    )
    return jax.shard_map(
        functools.partial(body, mesh.shape["row"], mesh.shape["col"]),
        mesh=mesh,
        in_specs=placed,
        out_specs=(P(None, None, "row", "col"), P()),
        check_vma=False,
    )
```

```python
import functools
import math

import jax
import jax.numpy as jnp
import ml_dtypes
import numpy as np
from jax import lax
from jax.experimental import pallas as pl
from jax.experimental.pallas import tpu as pltpu
from jax.sharding import PartitionSpec as P

EPS_AMP = 0.5
MESH = pl.DeviceIdType.MESH
N = 256
HALF = N // 2
MARGIN = 64
EXT = N + 2 * MARGIN
F32 = jnp.float32
BF16 = jnp.bfloat16


def dft_constants():
    j = np.arange(HALF)[:, None]
    k = np.arange(HALF)[None, :]
    mats = []
    for odd in (0, 1):
        angle = -2.0 * np.pi * (((2 * j + odd) * k) % N) / N
        re, im = np.cos(angle) / 16.0, np.sin(angle) / 16.0
        mats.append(np.block([[re, -im], [im, re]]))
    mats += [mats[0].T, mats[1].T]
    out = []
    for m in mats:
        hi = m.astype(ml_dtypes.bfloat16)
        lo = (m - hi.astype(np.float64)).astype(ml_dtypes.bfloat16)
        out.append(np.concatenate([hi, lo], axis=0))
    return np.stack(out)


def order_constant():
    q = np.zeros((N, N), np.float32)
    q[np.arange(HALF), 2 * np.arange(HALF)] = 1.0
    q[HALF + np.arange(HALF), 2 * np.arange(HALF) + 1] = 1.0
    return np.stack([q, q.T]).astype(ml_dtypes.bfloat16)


def dot(a, b):
    return jnp.dot(a, b, preferred_element_type=F32)


def two_terms(x):
    hi = x.astype(BF16)
    return hi, (x - hi.astype(F32)).astype(BF16)


def left_apply(table, x):
    hi, lo = two_terms(x)
    both = dot(table[...], hi)
    return both[:N] + both[N:] + dot(table[:N], lo)


def right_apply(x, table):
    hi, lo = two_terms(x)
    return dot(hi, table[:N]) + dot(lo, table[:N]) + dot(hi, table[N:])


def left_forward(x_re, x_im, tabs):
    low = jnp.concatenate([x_re[:HALF], x_im[:HALF]], axis=0)
    high = jnp.concatenate([x_re[HALF:], x_im[HALF:]], axis=0)
    even = left_apply(tabs.at[0], low + high)
    odd = left_apply(tabs.at[1], low - high)
    return (
        jnp.concatenate([even[:HALF], odd[:HALF]], axis=0),
        jnp.concatenate([even[HALF:], odd[HALF:]], axis=0),
    )


def right_forward(x_re, x_im, tabs):
    low = jnp.concatenate([x_re[:, :HALF], x_im[:, :HALF]], axis=1)
    high = jnp.concatenate([x_re[:, HALF:], x_im[:, HALF:]], axis=1)
    even = right_apply(low + high, tabs.at[2])
    odd = right_apply(low - high, tabs.at[3])
    return (
        jnp.concatenate([even[:, :HALF], odd[:, :HALF]], axis=1),
        jnp.concatenate([even[:, HALF:], odd[:, HALF:]], axis=1),
    )


def left_inverse(x_re, x_im, tabs):
    a = left_apply(tabs.at[2], jnp.concatenate([x_re[:HALF], x_im[:HALF]], axis=0))
    b = left_apply(tabs.at[3], jnp.concatenate([x_re[HALF:], x_im[HALF:]], axis=0))
    low, high = a + b, a - b
    return (
        jnp.concatenate([low[:HALF], high[:HALF]], axis=0),
        jnp.concatenate([low[HALF:], high[HALF:]], axis=0),
    )


def right_inverse(x_re, x_im, tabs):
    a = right_apply(jnp.concatenate([x_re[:, :HALF], x_im[:, :HALF]], axis=1), tabs.at[0])
    b = right_apply(jnp.concatenate([x_re[:, HALF:], x_im[:, HALF:]], axis=1), tabs.at[1])
    low, high = a + b, a - b
    return (
        jnp.concatenate([low[:, :HALF], high[:, :HALF]], axis=1),
        jnp.concatenate([low[:, HALF:], high[:, HALF:]], axis=1),
    )


def forward(x_re, x_im, tabs):
    return right_forward(*left_forward(x_re, x_im, tabs), tabs)


def inverse(x_re, x_im, tabs):
    return right_inverse(*left_inverse(x_re, x_im, tabs), tabs)


class Move:
    def __init__(self, copy, sends, arrives):
        self.copy, self.sends, self.arrives = copy, sends, arrives

    def start(self):
        pl.when(self.sends)(self.copy.start)

    def wait_send(self):
        pl.when(self.sends)(self.copy.wait_send)

    def wait_recv(self):
        pl.when(self.arrives)(self.copy.wait_recv)


def product(a_re, a_im, b_re, b_im):
    return a_re * b_re - a_im * b_im, a_re * b_im + a_im * b_re


def conj_product(a_re, a_im, b_re, b_im):
    return a_re * b_re + a_im * b_im, a_re * b_im - a_im * b_re


def reorder(x, order):
    hi = x.astype(BF16)
    rest = x - hi.astype(F32)
    mid = rest.astype(BF16)
    low = (rest - mid.astype(F32)).astype(BF16)
    parts = []
    for term in (hi, mid, low):
        rows = dot(order[0], term).astype(BF16)
        parts.append(dot(rows, order[1]))
    return parts[0] + parts[1] + parts[2]


def cos_sin(x):
    h = 0.5 * x
    t = h * h
    s = h * (1.0 + t * (-1.0 / 6 + t * (1.0 / 120 + t * (-1.0 / 5040 + t * (
        1.0 / 362880 + t * (-1.0 / 39916800 + t * (1.0 / 6227020800)))))))
    c = 1.0 + t * (-0.5 + t * (1.0 / 24 + t * (-1.0 / 720 + t * (1.0 / 40320 + t * (
        -1.0 / 3628800 + t * (1.0 / 479001600 + t * (-1.0 / 87178291200)))))))
    return 1.0 - 2.0 * s * s, 2.0 * s * c


def kernel(
    rows, cols,
    obj, probe_in, phase_in, amp_in, offs, tabs_in, order_in,
    obj_out, probe_out,
    mid, pack, hop, pick, side, probe, phase, amp, tabs, order, peer_offs, win1, win2, arrive, kern,
    gmid, gpick, gside, ghop, rrow, rhop, rcor, gprobe, recv_a, half, recv_b, sum_b, recv_c, final, owned,
    in_sem, offs_sem, halo_send, halo_recv, fold_send, fold_recv, ar_send, ar_recv, out_sem,
):
    row, col = lax.axis_index("row"), lax.axis_index("col")
    core, z_hi = row % 2, row // 2
    plane, z_lo = col // 2, col % 2
    planes, zs = cols // 2, rows
    z = z_hi * 2 + z_lo
    share = N // planes

    def neighbour(dr, dc):
        return ((row + dr + rows) % rows, (col + dc + cols) % cols)

    hop_to = 4 * z_lo - 2
    pair_peer = (row, col + 1 - 2 * z_lo)
    partner = (z_hi * 2 + 1 - core, col)

    side_len = math.isqrt(planes)
    far = lambda step, length: min(step, length - step)
    plane_steps = sorted(
        range(1, planes), key=lambda k: -far(k // side_len, side_len) - far(k % side_len, side_len))
    z_steps = sorted(range(1, zs), key=lambda k: -far(k, zs))

    def plane_at(k, sign=1):
        x, y = plane // side_len, plane % side_len
        return (x + side_len + sign * (k // side_len)) % side_len * side_len + (y + side_len + sign * (k % side_len)) % side_len

    def plane_peer(k):
        return (row, plane_at(k) * 2 + z_lo)

    def z_peer(k):
        other = (z + k) % zs
        return ((other // 2) * 2 + core, plane * 2 + other % 2)

    barrier = pltpu.get_barrier_semaphore()
    for step in ((-1, 0), (1, 0), (-1, -2), (-1, 2), (1, -2), (1, 2)):
        pl.semaphore_signal(barrier, inc=1, device_id=neighbour(*step), device_id_type=MESH)

    for k in plane_steps:
        pl.semaphore_signal(barrier, inc=1, device_id=plane_peer(k), device_id_type=MESH)
    for k in z_steps:
        pl.semaphore_signal(barrier, inc=1, device_id=z_peer(k), device_id_type=MESH)

    loads = [
        pltpu.make_async_copy(obj.at[0], mid.at[0, :, pl.ds(MARGIN, N), :], in_sem.at[0]),
        pltpu.make_async_copy(obj.at[1], mid.at[1, :, pl.ds(MARGIN, N), :], in_sem.at[1]),
        pltpu.make_async_copy(probe_in, probe, in_sem.at[2]),
        pltpu.make_async_copy(phase_in, phase, in_sem.at[3]),
        pltpu.make_async_copy(order_in, order, in_sem.at[4]),
        pltpu.make_async_copy(amp_in.at[0, 0, 0], amp, in_sem.at[5]),
        pltpu.make_async_copy(tabs_in, tabs, in_sem.at[6]),
    ]
    for load in loads:
        load.start()

    lane = lax.broadcasted_iota(jnp.int32, (N, HALF), 1)
    lower = lax.broadcasted_iota(jnp.int32, (EXT, HALF), 1) < 64

    def left_margin(re, im):
        return jnp.where(lower[:re.shape[0]], re, pltpu.roll(im, 64, 1))

    def right_margin(re, im):
        return jnp.where(lower[:re.shape[0]], pltpu.roll(re, 64, 1), im)

    def pack_outer(s):
        inner = pl.ds(MARGIN, N)

        @pl.when(z_lo == 0)
        def _():
            pack[s] = left_margin(mid[s, 0, inner, :HALF], mid[s, 1, inner, :HALF])

        @pl.when(z_lo == 1)
        def _():
            pack[s] = right_margin(mid[s, 0, inner, HALF:], mid[s, 1, inner, HALF:])

    def remote(src, dst, send, recv, device):
        return pltpu.make_async_remote_copy(
            src_ref=src, dst_ref=dst, send_sem=send, recv_sem=recv, device_id=device, device_id_type=MESH)

    def within(dr, dc):
        here, there = row + dr, col + dc
        return jnp.logical_and(
            jnp.logical_and(here >= 0, here < rows), jnp.logical_and(there >= 0, there < cols))

    def to_neighbour(src, dst, send, recv, dr, dc):
        return Move(remote(src, dst, send, recv, neighbour(dr, dc)), within(dr, dc), within(-dr, -dc))

    top, inner, bottom = pl.ds(0, MARGIN), pl.ds(MARGIN, N), pl.ds(MARGIN + N, MARGIN)

    def halo_hops(s):
        moves = (
            (pack.at[s], hop.at[s, inner, :], (0, hop_to)),
            (pack.at[s, pl.ds(0, MARGIN), :], hop.at[s, bottom, :], (-1, hop_to)),
            (pack.at[s, pl.ds(N - MARGIN, MARGIN), :], hop.at[s, top, :], (1, hop_to)),
        )
        return [to_neighbour(src, dst, halo_send.at[s, i], halo_recv.at[s, i], *step)
                for i, (src, dst, step) in enumerate(moves)]

    def halo_rows(s):
        moves = (
            (obj.at[s, :, pl.ds(0, MARGIN), :], mid.at[s, :, bottom, :], (-1, 0)),
            (obj.at[s, :, pl.ds(N - MARGIN, MARGIN), :], mid.at[s, :, top, :], (1, 0)),
        )
        return [to_neighbour(src, dst, halo_send.at[s, 3 + i], halo_recv.at[s, 3 + i], *step)
                for i, (src, dst, step) in enumerate(moves)]

    def halo_side(s):
        return remote(pick.at[s], side.at[s], halo_send.at[s, 5], halo_recv.at[s, 5], pair_peer)

    hops, halo_row, sides = ([f(s) for s in (0, 1)] for f in (halo_hops, halo_rows, halo_side))
    exchange = remote(offs, peer_offs, offs_sem.at[0], offs_sem.at[1], pair_peer)
    loads[0].wait()
    pack_outer(0)
    pl.semaphore_wait(barrier, 6 + planes - 1 + zs - 1)
    exchange.start()
    for copy in hops[0][1:] + halo_row[0] + hops[0][:1]:
        copy.start()
    loads[1].wait()
    pack_outer(1)
    hops[1][0].start()
    loads[3].wait()
    loads[4].wait()
    kern[0], kern[1] = cos_sin(reorder(phase[...], order))
    loads[5].wait()
    amp[...] = reorder(amp[...], order)
    loads[2].wait()
    loads[6].wait()

    @pl.when(jnp.logical_not(within(0, -hop_to)))
    def _():
        hop[...] = jnp.zeros_like(hop)

    for copy in halo_row[0]:
        copy.wait_send()
    for copy in hops[1][1:] + halo_row[1]:
        copy.start()
    off_y, off_x = offs[0, 0, 0, 0], offs[0, 0, 0, 1]
    shift = off_x - MARGIN

    outside = jnp.logical_or(
        jnp.logical_and(col == 0, off_x < MARGIN), jnp.logical_and(col == cols - 1, off_x > MARGIN))
    inside = 1.0 - outside.astype(F32)

    def clear_edges(s):
        @pl.when(row == 0)
        def _():
            mid[s, :, top, :] = jnp.zeros((2, MARGIN, N), F32)
            hop[s, top, :] = jnp.zeros((MARGIN, HALF), F32)

        @pl.when(row == rows - 1)
        def _():
            mid[s, :, bottom, :] = jnp.zeros((2, MARGIN, N), F32)
            hop[s, bottom, :] = jnp.zeros((MARGIN, HALF), F32)

    def up(x, amount):
        return pltpu.roll(x, lax.rem(EXT - amount, EXT), 0)[:N]

    def down(x, amount):
        below = jnp.zeros((EXT - N, x.shape[1]), F32)
        return pltpu.roll(jnp.concatenate([x, below], axis=0), amount, 0)

    def peer_takes_own(shape):
        reach = (peer_offs[0, 0, 0, 1] - MARGIN) * (1 - 2 * z_lo)
        return lax.broadcasted_iota(jnp.int32, shape, 1) * 0 + reach < 0

    def choose(s):
        own = peer_takes_own((EXT, HALF))

        @pl.when(z_lo == 0)
        def _():
            mine = right_margin(mid[s, 0, :, HALF:], mid[s, 1, :, HALF:])
            pick[s] = up(jnp.where(own, mine, hop[s]), peer_offs[0, 0, 0, 0])

        @pl.when(z_lo == 1)
        def _():
            mine = left_margin(mid[s, 0, :, :HALF], mid[s, 1, :, :HALF])
            pick[s] = up(jnp.where(own, mine, hop[s]), peer_offs[0, 0, 0, 0])

    over_right, over_left = lane < shift, lane >= HALF + shift

    def window(s, ref):
        beside = side[s] * inside
        turned = pltpu.roll(beside, 64, 1)
        for part in (0, 1):
            both = up(mid[s, part], off_y)
            low = jnp.where(over_right, beside if part == 0 else turned, both[:, :HALF])
            high = jnp.where(over_left, turned if part == 0 else beside, both[:, HALF:])
            ref[part] = pltpu.roll(jnp.concatenate([low, high], axis=1), lax.rem(N + MARGIN - off_x, N), 1)

    def spread(s, g_re, g_im):
        zero = jnp.zeros((N, HALF), F32)
        lefts, rights = [], []
        for part, g in ((0, g_re), (1, g_im)):
            moved = pltpu.roll(g, lax.rem(off_x + N - MARGIN, N), 1)
            low, high = moved[:, :HALF], moved[:, HALF:]
            rights.append(jnp.where(over_right, low, zero))
            lefts.append(jnp.where(over_left, high, zero))
            kept = [jnp.where(over_right, zero, low), jnp.where(over_left, zero, high)]
            gmid[s, part] = down(jnp.concatenate(kept, axis=1), off_y)
        gpick[s] = right_margin(*lefts) + left_margin(*rights)

    def fold_side(s):
        return remote(gpick.at[s], gside.at[s], fold_send.at[s, 5], fold_recv.at[s, 5], pair_peer)

    def fold_hops(s):
        moves = (
            (ghop.at[s, inner, :], rhop.at[s], (0, -hop_to)),
            (ghop.at[s, top, :], rcor.at[s, 0], (-1, -hop_to)),
            (ghop.at[s, bottom, :], rcor.at[s, 1], (1, -hop_to)),
        )
        return [to_neighbour(src, dst, fold_send.at[s, i], fold_recv.at[s, i], *step)
                for i, (src, dst, step) in enumerate(moves)]

    def fold_rows(s):
        moves = (
            (gmid.at[s, :, top, :], rrow.at[s, 0], (-1, 0)),
            (gmid.at[s, :, bottom, :], rrow.at[s, 1], (1, 0)),
        )
        return [to_neighbour(src, dst, fold_send.at[s, 3 + i], fold_recv.at[s, 3 + i], *step)
                for i, (src, dst, step) in enumerate(moves)]

    fsides, fhops, frows = ([f(s) for s in (0, 1)] for f in (fold_side, fold_hops, fold_rows))

    def add_packed(ref, s, place, packed, lefthand):
        low = lower[:packed.shape[0]]
        turned = pltpu.roll(packed, 64, 1)
        if lefthand:
            ref[s, 0, place, :HALF] += jnp.where(low, packed, 0.0)
            ref[s, 1, place, :HALF] += jnp.where(low, turned, 0.0)
        else:
            ref[s, 0, place, HALF:] += jnp.where(low, 0.0, turned)
            ref[s, 1, place, HALF:] += jnp.where(low, 0.0, packed)

    def pass_on(s):
        fsides[s].wait_recv()
        got = down(gside[s], peer_offs[0, 0, 0, 0])
        own = peer_takes_own((EXT, HALF))
        ghop[s] = jnp.where(own, 0.0, got)
        here = jnp.where(own, got, 0.0)

        @pl.when(z_lo == 0)
        def _():
            add_packed(gmid, s, pl.ds(0, EXT), here, False)

        @pl.when(z_lo == 1)
        def _():
            add_packed(gmid, s, pl.ds(0, EXT), here, True)

    first, last = pl.ds(0, MARGIN), pl.ds(N - MARGIN, MARGIN)

    def collect(s):
        for copy in fhops[s] + frows[s]:
            copy.wait_recv()
        for part in (0, 1):
            owned[s, part] = gmid[s, part, inner, :]

        @pl.when(row < rows - 1)
        def _():
            owned[s, :, last, :] += rrow[s, 0]

        @pl.when(row > 0)
        def _():
            owned[s, :, first, :] += rrow[s, 1]

        for lo, valid in ((0, col > 0), (1, col < cols - 1)):
            @pl.when(jnp.logical_and(z_lo == lo, valid))
            def _():
                add_packed(owned, s, pl.ds(0, N), rhop[s], lo == 0)

                @pl.when(row < rows - 1)
                def _():
                    add_packed(owned, s, last, rcor[s, 0], lo == 0)

                @pl.when(row > 0)
                def _():
                    add_packed(owned, s, first, rcor[s, 1], lo == 0)

    exchange.wait_recv()
    for copy in halo_row[0] + hops[0]:
        copy.wait_recv()
    clear_edges(0)
    choose(0)
    sides[0].start()
    for copy in halo_row[1] + hops[1]:
        copy.wait_recv()
    clear_edges(1)
    choose(1)
    sides[1].start()
    sides[0].wait_recv()
    window(0, win1)
    entry = product(probe[0], probe[1], win1[0], win1[1])
    spectrum = forward(*entry, tabs)
    moved = product(kern[0], kern[1], *spectrum)
    arrive[0], arrive[1] = inverse(*moved, tabs)

    sides[1].wait_recv()
    window(1, win2)
    far_re, far_im = forward(*product(arrive[0], arrive[1], win2[0], win2[1]), tabs)
    factor = 2.0 - 2.0 * amp[...] * lax.rsqrt(far_re * far_re + far_im * far_im + EPS_AMP)
    back_re, back_im = inverse(factor * far_re, factor * far_im, tabs)
    spread(1, *conj_product(arrive[0], arrive[1], back_re, back_im))
    fsides[1].start()
    spec = forward(*conj_product(win2[0], win2[1], back_re, back_im), tabs)
    ent_re, ent_im = inverse(*conj_product(kern[0], kern[1], *spec), tabs)
    gprobe[0], gprobe[1] = conj_product(win1[0], win1[1], ent_re, ent_im)

    both_cores = remote(gprobe.at[1 - core], recv_a, ar_send.at[0, 0], ar_recv.at[0, 0], partner)
    both_cores.start()
    spread(0, *conj_product(probe[0], probe[1], ent_re, ent_im))
    fsides[0].start()
    both_cores.wait_recv()
    half[...] = gprobe[core] + recv_a[...]

    def scatter(k):
        return remote(half.at[pl.ds(pl.multiple_of(plane_at(k) * share, share), share), :], recv_b.at[k],
                      ar_send.at[1, k], ar_recv.at[1, k], plane_peer(k))

    for k in plane_steps:
        scatter(k).start()
    mine = pl.ds(pl.multiple_of(plane * share, share), share)
    recv_b[0] = half[mine, :]
    pass_on(1)
    for copy in frows[1] + fhops[1][1:]:
        copy.start()
    for k in plane_steps:
        scatter(k).wait_recv()
    total = recv_b[0]
    for k in range(1, planes):
        total = total + recv_b[k]
    sum_b[...] = total

    def across(k):
        return remote(sum_b, recv_c.at[z], ar_send.at[2, k], ar_recv.at[2, k], z_peer(k))

    for k in z_steps:
        across(k).start()
    fhops[1][0].start()
    pass_on(0)
    fhops[0][0].start()
    for copy in frows[0] + fhops[0][1:]:
        copy.start()
    recv_c[z] = total
    for k in z_steps:
        across(k).wait_recv()
    total = recv_c[0]
    for d in range(1, zs):
        total = total + recv_c[d]
    final[mine, :] = total

    def gather(k):
        return remote(final.at[mine, :], final.at[mine, :], ar_send.at[3, k], ar_recv.at[3, k], plane_peer(k))

    def hand_over(k):
        place = pl.ds(pl.multiple_of(plane_at(k, -1) * share, share), share)
        return remote(final.at[place, :], probe_out.at[core, place, :], ar_send.at[4, k], ar_recv.at[4, k], partner)

    for k in plane_steps:
        gather(k).start()
    hand_over(0).start()
    for k in z_steps:
        across(k).wait_send()
    for s in (0, 1):
        for copy in [*hops[s], sides[s], fsides[s]]:
            copy.wait_send()
    for copy in halo_row[1] + fhops[1] + frows[1]:
        copy.wait_send()
    exchange.wait_send()
    both_cores.wait_send()
    for k in plane_steps:
        scatter(k).wait_send()
    collect(1)
    store1 = pltpu.make_async_copy(owned.at[1], obj_out.at[1], out_sem.at[1])
    store1.start()
    early = plane_steps[::-1][:10]
    for k in early:
        gather(k).wait_recv()
        hand_over(k).start()
    collect(0)
    store0 = pltpu.make_async_copy(owned.at[0], obj_out.at[0], out_sem.at[0])
    store0.start()
    for k in plane_steps[::-1][10:]:
        gather(k).wait_recv()
        hand_over(k).start()
    store2 = pltpu.make_async_copy(final, probe_out.at[core], out_sem.at[2])
    store2.start()
    for k in range(planes):
        hand_over(k).wait_recv()

    for copy in frows[0] + fhops[0]:
        copy.wait_send()
    for k in plane_steps:
        gather(k).wait_send()
    for k in range(planes):
        hand_over(k).wait_send()
    store0.wait()
    store1.wait()
    store2.wait()


def place_outputs(obj, probe, obj_out, probe_out, held, load_sem, store_sem):
    count = held.shape[0] // 6
    pieces = [pl.ds(i * (N // count), N // count) for i in range(count)]
    places = [(obj, obj_out, (i, j, piece)) for i in (0, 1) for j in (0, 1) for piece in pieces]
    places += [(probe, probe_out, (i, piece)) for i in (0, 1) for piece in pieces]
    loads = [pltpu.make_async_copy(src.at[at], held.at[k], load_sem.at[k]) for k, (src, _, at) in enumerate(places)]
    stores = [pltpu.make_async_copy(held.at[k], dst.at[at], store_sem.at[k]) for k, (_, dst, at) in enumerate(places)]
    for load in loads:
        load.start()
    for load, store in zip(loads, stores):
        load.wait()
        store.start()
    for store in stores:
        store.wait()


def body(rows, cols, object_field, probe, phase, amplitudes, offsets):
    planes, zs = cols // 2, rows
    share = N // planes
    vmem = lambda *shape: pltpu.VMEM(shape, F32)
    dma = pltpu.SemaphoreType.DMA
    hbm = pl.BlockSpec(memory_space=pl.ANY)
    grads = pl.pallas_call(
        functools.partial(kernel, rows, cols),
        out_shape=(
            jax.ShapeDtypeStruct((2, 2, N, N), F32),
            jax.ShapeDtypeStruct((2, N, N), F32),
        ),
        in_specs=[hbm, hbm, hbm, hbm, pl.BlockSpec(memory_space=pltpu.SMEM), hbm, hbm],
        out_specs=(hbm, hbm),
        scratch_shapes=[
            vmem(2, 2, EXT, N),
            vmem(2, N, HALF),
            vmem(2, EXT, HALF),
            vmem(2, N, HALF),
            vmem(2, N, HALF),
            vmem(2, N, N),
            vmem(N, N),
            vmem(N, N),
            pltpu.VMEM((4, 2 * N, N), BF16),
            pltpu.VMEM((2, N, N), BF16),
            pltpu.SMEM((1, 1, 1, 2), jnp.int32),
            vmem(2, N, N),
            vmem(2, N, N),
            vmem(2, N, N),
            vmem(2, N, N),
            vmem(2, 2, EXT, N),
            vmem(2, N, HALF),
            vmem(2, N, HALF),
            vmem(2, EXT, HALF),
            vmem(2, 2, 2, MARGIN, N),
            vmem(2, N, HALF),
            vmem(2, 2, MARGIN, HALF),
            vmem(2, N, N),
            vmem(N, N),
            vmem(N, N),
            vmem(planes, share, N),
            vmem(share, N),
            vmem(zs, share, N),
            vmem(N, N),
            vmem(2, 2, N, N),
            dma((7,)),
            dma((2,)),
            dma((2, 6)),
            dma((2, 6)),
            dma((2, 6)),
            dma((2, 6)),
            dma((5, 16)),
            dma((5, 16)),
            dma((3,)),
        ],
        compiler_params=pltpu.CompilerParams(
            collective_id=0, has_side_effects=True, vmem_limit_bytes=63 * 1024 * 1024
        ),
    )(object_field, probe, phase, amplitudes, offsets, jnp.asarray(dft_constants()), jnp.asarray(order_constant()))
    return pl.pallas_call(
        place_outputs,
        out_shape=(
            jax.ShapeDtypeStruct((2, 2, N, N), F32),
            jax.ShapeDtypeStruct((2, N, N), F32),
        ),
        in_specs=[hbm, hbm],
        out_specs=(hbm, hbm),
        scratch_shapes=[vmem(6 * 1, N // 1, N), dma((6 * 1,)), dma((6 * 1,))],
        compiler_params=pltpu.CompilerParams(vmem_limit_bytes=63 * 1024 * 1024),
    )(*grads)


def solution(mesh):
    placed = (
        P(None, None, "row", "col"),
        P(),
        P(),
        P("row", "col", None, None, None),
        P("row", "col", None, None),
    )
    return jax.shard_map(
        functools.partial(body, mesh.shape["row"], mesh.shape["col"]),
        mesh=mesh,
        in_specs=placed,
        out_specs=(P(None, None, "row", "col"), P()),
        check_vma=False,
    )
```

```python
import functools
import math

import jax
import jax.numpy as jnp
import ml_dtypes
import numpy as np
from jax import lax
from jax.experimental import pallas as pl
from jax.experimental.pallas import tpu as pltpu
from jax.sharding import PartitionSpec as P

EPS_AMP = 0.5
MESH = pl.DeviceIdType.MESH
N = 256
HALF = N // 2
MARGIN = 64
EXT = N + 2 * MARGIN
F32 = jnp.float32
BF16 = jnp.bfloat16


def dft_constants():
    j = np.arange(HALF)[:, None]
    k = np.arange(HALF)[None, :]
    mats = []
    for odd in (0, 1):
        angle = -2.0 * np.pi * (((2 * j + odd) * k) % N) / N
        re, im = np.cos(angle) / 16.0, np.sin(angle) / 16.0
        mats.append(np.block([[re, -im], [im, re]]))
    mats += [mats[0].T, mats[1].T]
    out = []
    for m in mats:
        hi = m.astype(ml_dtypes.bfloat16)
        lo = (m - hi.astype(np.float64)).astype(ml_dtypes.bfloat16)
        out.append(np.concatenate([hi, lo], axis=0))
    return np.stack(out)


def order_constant():
    q = np.zeros((N, N), np.float32)
    q[np.arange(HALF), 2 * np.arange(HALF)] = 1.0
    q[HALF + np.arange(HALF), 2 * np.arange(HALF) + 1] = 1.0
    return np.stack([q, q.T]).astype(ml_dtypes.bfloat16)


def dot(a, b):
    return jnp.dot(a, b, preferred_element_type=F32)


def two_terms(x):
    hi = x.astype(BF16)
    return hi, (x - hi.astype(F32)).astype(BF16)


def left_apply(table, x):
    hi, lo = two_terms(x)
    both = dot(table[...], hi)
    return both[:N] + both[N:] + dot(table[:N], lo)


def right_apply(x, table):
    hi, lo = two_terms(x)
    return dot(hi, table[:N]) + dot(lo, table[:N]) + dot(hi, table[N:])


def left_forward(x_re, x_im, tabs):
    low = jnp.concatenate([x_re[:HALF], x_im[:HALF]], axis=0)
    high = jnp.concatenate([x_re[HALF:], x_im[HALF:]], axis=0)
    even = left_apply(tabs.at[0], low + high)
    odd = left_apply(tabs.at[1], low - high)
    return (
        jnp.concatenate([even[:HALF], odd[:HALF]], axis=0),
        jnp.concatenate([even[HALF:], odd[HALF:]], axis=0),
    )


def right_forward(x_re, x_im, tabs):
    low = jnp.concatenate([x_re[:, :HALF], x_im[:, :HALF]], axis=1)
    high = jnp.concatenate([x_re[:, HALF:], x_im[:, HALF:]], axis=1)
    even = right_apply(low + high, tabs.at[2])
    odd = right_apply(low - high, tabs.at[3])
    return (
        jnp.concatenate([even[:, :HALF], odd[:, :HALF]], axis=1),
        jnp.concatenate([even[:, HALF:], odd[:, HALF:]], axis=1),
    )


def left_inverse(x_re, x_im, tabs):
    a = left_apply(tabs.at[2], jnp.concatenate([x_re[:HALF], x_im[:HALF]], axis=0))
    b = left_apply(tabs.at[3], jnp.concatenate([x_re[HALF:], x_im[HALF:]], axis=0))
    low, high = a + b, a - b
    return (
        jnp.concatenate([low[:HALF], high[:HALF]], axis=0),
        jnp.concatenate([low[HALF:], high[HALF:]], axis=0),
    )


def right_inverse(x_re, x_im, tabs):
    a = right_apply(jnp.concatenate([x_re[:, :HALF], x_im[:, :HALF]], axis=1), tabs.at[0])
    b = right_apply(jnp.concatenate([x_re[:, HALF:], x_im[:, HALF:]], axis=1), tabs.at[1])
    low, high = a + b, a - b
    return (
        jnp.concatenate([low[:, :HALF], high[:, :HALF]], axis=1),
        jnp.concatenate([low[:, HALF:], high[:, HALF:]], axis=1),
    )


def forward(x_re, x_im, tabs):
    return right_forward(*left_forward(x_re, x_im, tabs), tabs)


def inverse(x_re, x_im, tabs):
    return right_inverse(*left_inverse(x_re, x_im, tabs), tabs)


class Move:
    def __init__(self, copy, sends, arrives):
        self.copy, self.sends, self.arrives = copy, sends, arrives

    def start(self):
        pl.when(self.sends)(self.copy.start)

    def wait_send(self):
        pl.when(self.sends)(self.copy.wait_send)

    def wait_recv(self):
        pl.when(self.arrives)(self.copy.wait_recv)


def product(a_re, a_im, b_re, b_im):
    return a_re * b_re - a_im * b_im, a_re * b_im + a_im * b_re


def conj_product(a_re, a_im, b_re, b_im):
    return a_re * b_re + a_im * b_im, a_re * b_im - a_im * b_re


def reorder(x, order):
    hi = x.astype(BF16)
    rest = x - hi.astype(F32)
    mid = rest.astype(BF16)
    low = (rest - mid.astype(F32)).astype(BF16)
    parts = []
    for term in (hi, mid, low):
        rows = dot(order[0], term).astype(BF16)
        parts.append(dot(rows, order[1]))
    return parts[0] + parts[1] + parts[2]


def cos_sin(x):
    h = 0.5 * x
    t = h * h
    s = h * (1.0 + t * (-1.0 / 6 + t * (1.0 / 120 + t * (-1.0 / 5040 + t * (
        1.0 / 362880 + t * (-1.0 / 39916800 + t * (1.0 / 6227020800)))))))
    c = 1.0 + t * (-0.5 + t * (1.0 / 24 + t * (-1.0 / 720 + t * (1.0 / 40320 + t * (
        -1.0 / 3628800 + t * (1.0 / 479001600 + t * (-1.0 / 87178291200)))))))
    return 1.0 - 2.0 * s * s, 2.0 * s * c


def kernel(
    rows, cols,
    obj, probe_in, phase_in, amp_in, offs, tabs_in, order_in,
    obj_out, probe_out,
    mid, pack, hop, pick, side, probe, phase, amp, tabs, order, peer_offs, win1, win2, arrive, kern,
    gmid, gpick, gside, ghop, rrow, rhop, rcor, gprobe, recv_a, half, recv_b, sum_b, recv_c, final, owned,
    in_sem, offs_sem, halo_send, halo_recv, fold_send, fold_recv, ar_send, ar_recv, out_sem,
):
    row, col = lax.axis_index("row"), lax.axis_index("col")
    core, z_hi = row % 2, row // 2
    plane, z_lo = col // 2, col % 2
    planes, zs = cols // 2, rows
    z = z_hi * 2 + z_lo
    share = N // planes

    def neighbour(dr, dc):
        return ((row + dr + rows) % rows, (col + dc + cols) % cols)

    hop_to = 4 * z_lo - 2
    pair_peer = (row, col + 1 - 2 * z_lo)
    partner = (z_hi * 2 + 1 - core, col)

    side_len = math.isqrt(planes)
    far = lambda step, length: min(step, length - step)
    plane_steps = sorted(
        range(1, planes), key=lambda k: -far(k // side_len, side_len) - far(k % side_len, side_len))
    z_steps = sorted(range(1, zs), key=lambda k: -far(k, zs))

    def plane_at(k, sign=1):
        x, y = plane // side_len, plane % side_len
        return (x + side_len + sign * (k // side_len)) % side_len * side_len + (y + side_len + sign * (k % side_len)) % side_len

    def plane_peer(k):
        return (row, plane_at(k) * 2 + z_lo)

    def z_peer(k):
        other = (z + k) % zs
        return ((other // 2) * 2 + core, plane * 2 + other % 2)

    barrier = pltpu.get_barrier_semaphore()
    for step in ((-1, 0), (1, 0), (-1, -2), (-1, 2), (1, -2), (1, 2)):
        pl.semaphore_signal(barrier, inc=1, device_id=neighbour(*step), device_id_type=MESH)

    for k in plane_steps:
        pl.semaphore_signal(barrier, inc=1, device_id=plane_peer(k), device_id_type=MESH)
    for k in z_steps:
        pl.semaphore_signal(barrier, inc=1, device_id=z_peer(k), device_id_type=MESH)

    loads = [
        pltpu.make_async_copy(obj.at[0], mid.at[0, :, pl.ds(MARGIN, N), :], in_sem.at[0]),
        pltpu.make_async_copy(obj.at[1], mid.at[1, :, pl.ds(MARGIN, N), :], in_sem.at[1]),
        pltpu.make_async_copy(probe_in, probe, in_sem.at[2]),
        pltpu.make_async_copy(phase_in, phase, in_sem.at[3]),
        pltpu.make_async_copy(order_in, order, in_sem.at[4]),
        pltpu.make_async_copy(amp_in.at[0, 0, 0], amp, in_sem.at[5]),
        pltpu.make_async_copy(tabs_in, tabs, in_sem.at[6]),
    ]
    for load in loads:
        load.start()

    lane = lax.broadcasted_iota(jnp.int32, (N, HALF), 1)
    lower = lax.broadcasted_iota(jnp.int32, (EXT, HALF), 1) < 64

    def left_margin(re, im):
        return jnp.where(lower[:re.shape[0]], re, pltpu.roll(im, 64, 1))

    def right_margin(re, im):
        return jnp.where(lower[:re.shape[0]], pltpu.roll(re, 64, 1), im)

    def pack_outer(s):
        inner = pl.ds(MARGIN, N)

        @pl.when(z_lo == 0)
        def _():
            pack[s] = left_margin(mid[s, 0, inner, :HALF], mid[s, 1, inner, :HALF])

        @pl.when(z_lo == 1)
        def _():
            pack[s] = right_margin(mid[s, 0, inner, HALF:], mid[s, 1, inner, HALF:])

    def remote(src, dst, send, recv, device):
        return pltpu.make_async_remote_copy(
            src_ref=src, dst_ref=dst, send_sem=send, recv_sem=recv, device_id=device, device_id_type=MESH)

    def within(dr, dc):
        here, there = row + dr, col + dc
        return jnp.logical_and(
            jnp.logical_and(here >= 0, here < rows), jnp.logical_and(there >= 0, there < cols))

    def to_neighbour(src, dst, send, recv, dr, dc):
        return Move(remote(src, dst, send, recv, neighbour(dr, dc)), within(dr, dc), within(-dr, -dc))

    top, inner, bottom = pl.ds(0, MARGIN), pl.ds(MARGIN, N), pl.ds(MARGIN + N, MARGIN)

    def halo_hops(s):
        moves = (
            (pack.at[s], hop.at[s, inner, :], (0, hop_to)),
            (pack.at[s, pl.ds(0, MARGIN), :], hop.at[s, bottom, :], (-1, hop_to)),
            (pack.at[s, pl.ds(N - MARGIN, MARGIN), :], hop.at[s, top, :], (1, hop_to)),
        )
        return [to_neighbour(src, dst, halo_send.at[s, i], halo_recv.at[s, i], *step)
                for i, (src, dst, step) in enumerate(moves)]

    def halo_rows(s):
        moves = (
            (obj.at[s, :, pl.ds(0, MARGIN), :], mid.at[s, :, bottom, :], (-1, 0)),
            (obj.at[s, :, pl.ds(N - MARGIN, MARGIN), :], mid.at[s, :, top, :], (1, 0)),
        )
        return [to_neighbour(src, dst, halo_send.at[s, 3 + i], halo_recv.at[s, 3 + i], *step)
                for i, (src, dst, step) in enumerate(moves)]

    def halo_side(s):
        return remote(pick.at[s], side.at[s], halo_send.at[s, 5], halo_recv.at[s, 5], pair_peer)

    hops, halo_row, sides = ([f(s) for s in (0, 1)] for f in (halo_hops, halo_rows, halo_side))
    exchange = remote(offs, peer_offs, offs_sem.at[0], offs_sem.at[1], pair_peer)
    loads[0].wait()
    pack_outer(0)
    pl.semaphore_wait(barrier, 6 + planes - 1 + zs - 1)
    exchange.start()
    for copy in hops[0][1:] + halo_row[0] + hops[0][:1]:
        copy.start()
    loads[1].wait()
    pack_outer(1)
    hops[1][0].start()
    loads[3].wait()
    loads[4].wait()
    kern[0], kern[1] = cos_sin(reorder(phase[...], order))
    loads[5].wait()
    amp[...] = reorder(amp[...], order)
    loads[2].wait()
    loads[6].wait()

    @pl.when(jnp.logical_not(within(0, -hop_to)))
    def _():
        hop[...] = jnp.zeros_like(hop)

    for copy in halo_row[0]:
        copy.wait_send()
    for copy in hops[1][1:] + halo_row[1]:
        copy.start()
    off_y, off_x = offs[0, 0, 0, 0], offs[0, 0, 0, 1]
    shift = off_x - MARGIN

    outside = jnp.logical_or(
        jnp.logical_and(col == 0, off_x < MARGIN), jnp.logical_and(col == cols - 1, off_x > MARGIN))
    inside = 1.0 - outside.astype(F32)

    def clear_edges(s):
        @pl.when(row == 0)
        def _():
            mid[s, :, top, :] = jnp.zeros((2, MARGIN, N), F32)
            hop[s, top, :] = jnp.zeros((MARGIN, HALF), F32)

        @pl.when(row == rows - 1)
        def _():
            mid[s, :, bottom, :] = jnp.zeros((2, MARGIN, N), F32)
            hop[s, bottom, :] = jnp.zeros((MARGIN, HALF), F32)

    def up(x, amount):
        return pltpu.roll(x, lax.rem(EXT - amount, EXT), 0)[:N]

    def down(x, amount):
        below = jnp.zeros((EXT - N, x.shape[1]), F32)
        return pltpu.roll(jnp.concatenate([x, below], axis=0), amount, 0)

    def peer_takes_own(shape):
        reach = (peer_offs[0, 0, 0, 1] - MARGIN) * (1 - 2 * z_lo)
        return lax.broadcasted_iota(jnp.int32, shape, 1) * 0 + reach < 0

    def choose(s):
        own = peer_takes_own((EXT, HALF))

        @pl.when(z_lo == 0)
        def _():
            mine = right_margin(mid[s, 0, :, HALF:], mid[s, 1, :, HALF:])
            pick[s] = up(jnp.where(own, mine, hop[s]), peer_offs[0, 0, 0, 0])

        @pl.when(z_lo == 1)
        def _():
            mine = left_margin(mid[s, 0, :, :HALF], mid[s, 1, :, :HALF])
            pick[s] = up(jnp.where(own, mine, hop[s]), peer_offs[0, 0, 0, 0])

    over_right, over_left = lane < shift, lane >= HALF + shift

    def window(s, ref):
        beside = side[s] * inside
        turned = pltpu.roll(beside, 64, 1)
        for part in (0, 1):
            both = up(mid[s, part], off_y)
            low = jnp.where(over_right, beside if part == 0 else turned, both[:, :HALF])
            high = jnp.where(over_left, turned if part == 0 else beside, both[:, HALF:])
            ref[part] = pltpu.roll(jnp.concatenate([low, high], axis=1), lax.rem(N + MARGIN - off_x, N), 1)

    def spread(s, g_re, g_im):
        zero = jnp.zeros((N, HALF), F32)
        lefts, rights = [], []
        for part, g in ((0, g_re), (1, g_im)):
            moved = pltpu.roll(g, lax.rem(off_x + N - MARGIN, N), 1)
            low, high = moved[:, :HALF], moved[:, HALF:]
            rights.append(jnp.where(over_right, low, zero))
            lefts.append(jnp.where(over_left, high, zero))
            kept = [jnp.where(over_right, zero, low), jnp.where(over_left, zero, high)]
            gmid[s, part] = down(jnp.concatenate(kept, axis=1), off_y)
        gpick[s] = right_margin(*lefts) + left_margin(*rights)

    def fold_side(s):
        return remote(gpick.at[s], gside.at[s], fold_send.at[s, 5], fold_recv.at[s, 5], pair_peer)

    def fold_hops(s):
        moves = (
            (ghop.at[s, inner, :], rhop.at[s], (0, -hop_to)),
            (ghop.at[s, top, :], rcor.at[s, 0], (-1, -hop_to)),
            (ghop.at[s, bottom, :], rcor.at[s, 1], (1, -hop_to)),
        )
        return [to_neighbour(src, dst, fold_send.at[s, i], fold_recv.at[s, i], *step)
                for i, (src, dst, step) in enumerate(moves)]

    def fold_rows(s):
        moves = (
            (gmid.at[s, :, top, :], rrow.at[s, 0], (-1, 0)),
            (gmid.at[s, :, bottom, :], rrow.at[s, 1], (1, 0)),
        )
        return [to_neighbour(src, dst, fold_send.at[s, 3 + i], fold_recv.at[s, 3 + i], *step)
                for i, (src, dst, step) in enumerate(moves)]

    fsides, fhops, frows = ([f(s) for s in (0, 1)] for f in (fold_side, fold_hops, fold_rows))

    def add_packed(ref, s, place, packed, lefthand):
        low = lower[:packed.shape[0]]
        turned = pltpu.roll(packed, 64, 1)
        if lefthand:
            ref[s, 0, place, :HALF] += jnp.where(low, packed, 0.0)
            ref[s, 1, place, :HALF] += jnp.where(low, turned, 0.0)
        else:
            ref[s, 0, place, HALF:] += jnp.where(low, 0.0, turned)
            ref[s, 1, place, HALF:] += jnp.where(low, 0.0, packed)

    def pass_on(s):
        fsides[s].wait_recv()
        got = down(gside[s], peer_offs[0, 0, 0, 0])
        own = peer_takes_own((EXT, HALF))
        ghop[s] = jnp.where(own, 0.0, got)
        here = jnp.where(own, got, 0.0)

        @pl.when(z_lo == 0)
        def _():
            add_packed(gmid, s, pl.ds(0, EXT), here, False)

        @pl.when(z_lo == 1)
        def _():
            add_packed(gmid, s, pl.ds(0, EXT), here, True)

    first, last = pl.ds(0, MARGIN), pl.ds(N - MARGIN, MARGIN)

    def collect(s):
        for copy in fhops[s] + frows[s]:
            copy.wait_recv()
        for part in (0, 1):
            owned[s, part] = gmid[s, part, inner, :]

        @pl.when(row < rows - 1)
        def _():
            owned[s, :, last, :] += rrow[s, 0]

        @pl.when(row > 0)
        def _():
            owned[s, :, first, :] += rrow[s, 1]

        for lo, valid in ((0, col > 0), (1, col < cols - 1)):
            @pl.when(jnp.logical_and(z_lo == lo, valid))
            def _():
                add_packed(owned, s, pl.ds(0, N), rhop[s], lo == 0)

                @pl.when(row < rows - 1)
                def _():
                    add_packed(owned, s, last, rcor[s, 0], lo == 0)

                @pl.when(row > 0)
                def _():
                    add_packed(owned, s, first, rcor[s, 1], lo == 0)

    exchange.wait_recv()
    for copy in halo_row[0] + hops[0]:
        copy.wait_recv()
    clear_edges(0)
    choose(0)
    sides[0].start()
    for copy in halo_row[1] + hops[1]:
        copy.wait_recv()
    clear_edges(1)
    choose(1)
    sides[1].start()
    sides[0].wait_recv()
    window(0, win1)
    entry = product(probe[0], probe[1], win1[0], win1[1])
    spectrum = forward(*entry, tabs)
    moved = product(kern[0], kern[1], *spectrum)
    arrive[0], arrive[1] = inverse(*moved, tabs)

    sides[1].wait_recv()
    window(1, win2)
    far_re, far_im = forward(*product(arrive[0], arrive[1], win2[0], win2[1]), tabs)
    factor = 2.0 - 2.0 * amp[...] * lax.rsqrt(far_re * far_re + far_im * far_im + EPS_AMP)
    back_re, back_im = inverse(factor * far_re, factor * far_im, tabs)
    spread(1, *conj_product(arrive[0], arrive[1], back_re, back_im))
    fsides[1].start()
    spec = forward(*conj_product(win2[0], win2[1], back_re, back_im), tabs)
    ent_re, ent_im = inverse(*conj_product(kern[0], kern[1], *spec), tabs)
    gprobe[0], gprobe[1] = conj_product(win1[0], win1[1], ent_re, ent_im)

    both_cores = remote(gprobe.at[1 - core], recv_a, ar_send.at[0, 0], ar_recv.at[0, 0], partner)
    both_cores.start()
    spread(0, *conj_product(probe[0], probe[1], ent_re, ent_im))
    fsides[0].start()
    both_cores.wait_recv()
    half[...] = gprobe[core] + recv_a[...]

    def scatter(k):
        return remote(half.at[pl.ds(pl.multiple_of(plane_at(k) * share, share), share), :], recv_b.at[k],
                      ar_send.at[1, k], ar_recv.at[1, k], plane_peer(k))

    for k in plane_steps:
        scatter(k).start()
    mine = pl.ds(pl.multiple_of(plane * share, share), share)
    recv_b[0] = half[mine, :]
    pass_on(1)
    for copy in frows[1] + fhops[1][1:]:
        copy.start()
    for k in plane_steps:
        scatter(k).wait_recv()
    total = recv_b[0]
    for k in range(1, planes):
        total = total + recv_b[k]
    sum_b[...] = total

    def across(k):
        return remote(sum_b, recv_c.at[z], ar_send.at[2, k], ar_recv.at[2, k], z_peer(k))

    for k in z_steps:
        across(k).start()
    fhops[1][0].start()
    pass_on(0)
    fhops[0][0].start()
    for copy in frows[0] + fhops[0][1:]:
        copy.start()
    recv_c[z] = total
    for k in z_steps:
        across(k).wait_recv()
    total = recv_c[0]
    for d in range(1, zs):
        total = total + recv_c[d]
    final[mine, :] = total

    def gather(k):
        return remote(final.at[mine, :], final.at[mine, :], ar_send.at[3, k], ar_recv.at[3, k], plane_peer(k))

    def hand_over(k):
        place = pl.ds(pl.multiple_of(plane_at(k, -1) * share, share), share)
        return remote(final.at[place, :], probe_out.at[core, place, :], ar_send.at[4, k], ar_recv.at[4, k], partner)

    for k in plane_steps:
        gather(k).start()
    hand_over(0).start()
    for k in z_steps:
        across(k).wait_send()
    for s in (0, 1):
        for copy in [*hops[s], sides[s], fsides[s]]:
            copy.wait_send()
    for copy in halo_row[1] + fhops[1] + frows[1]:
        copy.wait_send()
    exchange.wait_send()
    both_cores.wait_send()
    for k in plane_steps:
        scatter(k).wait_send()
    collect(1)
    store1 = pltpu.make_async_copy(owned.at[1], obj_out.at[1], out_sem.at[1])
    store1.start()
    collect(0)
    store0 = pltpu.make_async_copy(owned.at[0], obj_out.at[0], out_sem.at[0])
    store0.start()
    for copy in frows[0] + fhops[0]:
        copy.wait_send()
    for k in plane_steps[::-1]:
        gather(k).wait_recv()
        hand_over(k).start()
    store2 = pltpu.make_async_copy(final, probe_out.at[core], out_sem.at[2])
    store2.start()
    for k in range(planes):
        hand_over(k).wait_recv()

    for k in plane_steps:
        gather(k).wait_send()
    for k in range(planes):
        hand_over(k).wait_send()
    store0.wait()
    store1.wait()
    store2.wait()


def place_outputs(obj, probe, obj_out, probe_out, held, load_sem, store_sem):
    count = held.shape[0] // 6
    pieces = [pl.ds(i * (N // count), N // count) for i in range(count)]
    places = [(obj, obj_out, (i, j, piece)) for i in (0, 1) for j in (0, 1) for piece in pieces]
    places += [(probe, probe_out, (i, piece)) for i in (0, 1) for piece in pieces]
    loads = [pltpu.make_async_copy(src.at[at], held.at[k], load_sem.at[k]) for k, (src, _, at) in enumerate(places)]
    stores = [pltpu.make_async_copy(held.at[k], dst.at[at], store_sem.at[k]) for k, (_, dst, at) in enumerate(places)]
    for load in loads:
        load.start()
    for load, store in zip(loads, stores):
        load.wait()
        store.start()
    for store in stores:
        store.wait()


def body(rows, cols, object_field, probe, phase, amplitudes, offsets):
    planes, zs = cols // 2, rows
    share = N // planes
    vmem = lambda *shape: pltpu.VMEM(shape, F32)
    dma = pltpu.SemaphoreType.DMA
    hbm = pl.BlockSpec(memory_space=pl.ANY)
    grads = pl.pallas_call(
        functools.partial(kernel, rows, cols),
        out_shape=(
            jax.ShapeDtypeStruct((2, 2, N, N), F32),
            jax.ShapeDtypeStruct((2, N, N), F32),
        ),
        in_specs=[hbm, hbm, hbm, hbm, pl.BlockSpec(memory_space=pltpu.SMEM), hbm, hbm],
        out_specs=(hbm, hbm),
        scratch_shapes=[
            vmem(2, 2, EXT, N),
            vmem(2, N, HALF),
            vmem(2, EXT, HALF),
            vmem(2, N, HALF),
            vmem(2, N, HALF),
            vmem(2, N, N),
            vmem(N, N),
            vmem(N, N),
            pltpu.VMEM((4, 2 * N, N), BF16),
            pltpu.VMEM((2, N, N), BF16),
            pltpu.SMEM((1, 1, 1, 2), jnp.int32),
            vmem(2, N, N),
            vmem(2, N, N),
            vmem(2, N, N),
            vmem(2, N, N),
            vmem(2, 2, EXT, N),
            vmem(2, N, HALF),
            vmem(2, N, HALF),
            vmem(2, EXT, HALF),
            vmem(2, 2, 2, MARGIN, N),
            vmem(2, N, HALF),
            vmem(2, 2, MARGIN, HALF),
            vmem(2, N, N),
            vmem(N, N),
            vmem(N, N),
            vmem(planes, share, N),
            vmem(share, N),
            vmem(zs, share, N),
            vmem(N, N),
            vmem(2, 2, N, N),
            dma((7,)),
            dma((2,)),
            dma((2, 6)),
            dma((2, 6)),
            dma((2, 6)),
            dma((2, 6)),
            dma((5, 16)),
            dma((5, 16)),
            dma((3,)),
        ],
        compiler_params=pltpu.CompilerParams(
            collective_id=0, has_side_effects=True, vmem_limit_bytes=63 * 1024 * 1024
        ),
    )(object_field, probe, phase, amplitudes, offsets, jnp.asarray(dft_constants()), jnp.asarray(order_constant()))
    return pl.pallas_call(
        place_outputs,
        out_shape=(
            jax.ShapeDtypeStruct((2, 2, N, N), F32),
            jax.ShapeDtypeStruct((2, N, N), F32),
        ),
        in_specs=[hbm, hbm],
        out_specs=(hbm, hbm),
        scratch_shapes=[vmem(6 * 1, N // 1, N), dma((6 * 1,)), dma((6 * 1,))],
        compiler_params=pltpu.CompilerParams(vmem_limit_bytes=63 * 1024 * 1024),
    )(*grads)


def solution(mesh):
    placed = (
        P(None, None, "row", "col"),
        P(),
        P(),
        P("row", "col", None, None, None),
        P("row", "col", None, None),
    )
    return jax.shard_map(
        functools.partial(body, mesh.shape["row"], mesh.shape["col"]),
        mesh=mesh,
        in_specs=placed,
        out_specs=(P(None, None, "row", "col"), P()),
        check_vma=False,
    )
```
